32 devices in a mesh: dp: 8 (over z, y), tensor: 4 (over x, core).
Axes of the slice: x: 2, y: 2, z: 4, core: 2. Of those that a mesh axis runs over, the one named last changes fastest.
Arguments:
- token_ids: int32 [256, 512], P('dp'), may hold values from 0 to 31999
- lengths: int32 [256], P('dp'), may hold values from 128 to 512
- table: bfloat16 [1024, 32000], P('tensor'), may hold values from -6 to 6
- cotangent: bfloat16 [256, 1024, 256], P('dp', 'tensor'), may hold values from -6 to 6
- proj_a: bfloat16 [1024, 64], P('tensor'), may hold values from -0.1875 to 0.1875
- proj_b: bfloat16 [1024, 5, 64], P('tensor'), may hold values from -0.078125 to 0.078125
Outputs:
- similarity: float32 [256, 256], P(('dp', 'tensor'))
The draws below stay inside these ranges and needn't reach their ends.
Inputs may be any that keep to these rules, and one draw needn't show every extreme that they name: `lengths`: each recipe has at least a quarter of its positions live.
All inputs are finite; a program needn't handle non-finite values.
Results may differ from the reference program's by a relative error of at most 0.0012.
Values may be sent and summed in bfloat16 or wider, within the bound.
A program may use at most 320 MiB of HBM per device.

```python
import math
import jax
import jax.numpy as jnp
import numpy as np
from jax import lax

CH = 1024
KERNEL = 5
PROJ = 64
VOCAB = 32000
SEQ = 512
T_OUT = 256
FEATS = 4096
RECIPES = 256


def touch_ends(drawn, stream_key, smallest, top_value):
    longest = drawn.shape.index(max(drawn.shape))
    spots = []
    for shift in (0, 1):
        where = [jax.random.randint(jax.random.fold_in(stream_key, axis), (), 0, length) for axis, length in enumerate(drawn.shape)]
        where[longest] = (where[longest] + shift) % drawn.shape[longest]
        spots.append(tuple(where))
    return drawn.at[spots[0]].set(smallest).at[spots[1]].set(top_value)


def block_levels(key, dims, shards, smallest, top_value):
    gain, own = 1.0, jax.random.fold_in(key, 6)
    for axis_at, blocks in shards:
        heights = jnp.exp(jax.random.uniform(jax.random.fold_in(own, axis_at), (blocks,), jnp.float32, smallest / len(shards), top_value / len(shards)))
        gain = gain * jnp.repeat(heights, dims[axis_at] // blocks).reshape([-1 if axis == axis_at else 1 for axis in range(len(dims))])
    return gain


def rank_bounds(amount, slope):
    portions = [(1 << 20) // math.isqrt(grade ** slope) + 1 for grade in range(1, amount + 1)]
    deviation = 1 + sum(portions) // (1 << 30)
    return np.cumsum(np.array([max(1, weight // deviation) for weight in portions]))


def ranked_ids(own_key, dims, number_of, slope):
    table = rank_bounds(number_of, slope)
    pick = jax.random.randint(jax.random.fold_in(own_key, 1), dims, 0, int(table[number_of - 1]))
    grade = jnp.searchsorted(jnp.asarray(table, jnp.int32), pick, side="right")
    return jax.random.permutation(jax.random.fold_in(own_key, 2), number_of)[grade].astype(jnp.int32)


def normal_values(own_key, extent, width, limit, split=(), kind=jnp.bfloat16):
    loudness = block_levels(own_key, extent, split, -0.22, 0.18) if split else 1.0
    drawn = jax.random.normal(own_key, extent, jnp.float32) * width * loudness
    return jnp.minimum(jnp.maximum(drawn, -limit), limit).astype(kind)


def setup_inputs(seed: int = 0) -> dict:
    arg_keys = jax.random.split(jax.random.key(seed), 7)
    token_ids = touch_ends(ranked_ids(arg_keys[0], (RECIPES, SEQ), VOCAB, 2), jax.random.fold_in(arg_keys[0], 3), 0, VOCAB - 1).astype(jnp.int32)
    lengths = touch_ends(jax.random.randint(arg_keys[1], (RECIPES,), SEQ // 4, SEQ + 1), jax.random.fold_in(arg_keys[1], 1), SEQ // 4, SEQ).astype(jnp.int32)
    table = normal_values(arg_keys[2], (CH, VOCAB), 1.0, 6.0, ((0, 4),))
    cotangent = normal_values(arg_keys[3], (RECIPES, CH, T_OUT), 1.0, 6.0, ((0, 8), (1, 4)))
    proj_a = normal_values(arg_keys[4], (CH, PROJ), CH ** -0.5, 0.1875, ((0, 4),))
    proj_b = normal_values(arg_keys[5], (CH, KERNEL, PROJ), (CH * KERNEL) ** -0.5, 0.078125, ((0, 4),))
    return dict(token_ids=token_ids, lengths=lengths, table=table, cotangent=cotangent, proj_a=proj_a, proj_b=proj_b)


def block_features(ids_b, len_b, delta_b, table, proj_a, proj_b):
    count = ids_b.shape[0]
    pos = jnp.arange(SEQ, dtype=jnp.int32)
    keep = (pos[None, :] < len_b[:, None]).astype(table.dtype)
    embedded = jnp.take(table, ids_b, axis=1) * keep[None, :, :]
    padded = jnp.pad(embedded, ((0, 0), (0, 0), (KERNEL // 2, KERNEL // 2)))
    right = jnp.zeros((count, PROJ, T_OUT), jnp.float32)
    for k in range(KERNEL):
        tap = padded[:, :, k:k + SEQ:2]
        right = right + jnp.einsum('cnt,cb->nbt', tap.astype(jnp.float32), proj_b[:, k, :].astype(jnp.float32))
    outpos = 2 * jnp.arange(T_OUT, dtype=jnp.int32)
    tkeep = (outpos[None, :] < len_b[:, None]).astype(delta_b.dtype)
    masked = delta_b * tkeep[:, None, :]
    left = jnp.einsum('nct,ca->nat', masked.astype(jnp.float32), proj_a.astype(jnp.float32))
    raw = jnp.einsum('nat,nbt->nab', left, right, precision=lax.Precision.HIGHEST).reshape(count, FEATS)
    scale = lax.rsqrt(lax.optimization_barrier(jnp.mean(raw * raw, axis=1)) + 1e-06)
    return (raw * scale[:, None]).astype(jnp.bfloat16)

def reference(token_ids, lengths, table, cotangent, proj_a, proj_b):
    blocks = min(32, RECIPES)
    nblk = RECIPES // blocks
    ids_r = token_ids.reshape(nblk, blocks, SEQ)
    len_r = lengths.reshape(nblk, blocks)
    del_r = cotangent.reshape(nblk, blocks, CH, T_OUT)

    def one(parts):
        return block_features(parts[0], parts[1], parts[2], table, proj_a, proj_b)
    unit = lax.map(one, (ids_r, len_r, del_r)).reshape(RECIPES, FEATS)
    return jnp.dot(unit, unit.T, preferred_element_type=jnp.float32) * (1.0 / FEATS)
```

```python
import functools

import jax
import jax.numpy as jnp
from jax import lax
from jax.experimental import pallas as pl
from jax.experimental.pallas import tpu as pltpu
from jax.sharding import PartitionSpec as P

LANES = 128
UNROLL = 32
PAD = 32
CHUNK = 640


def right_kernel(vocab, vblocks, group, steps_out, ids_ref, live_ref, table_ref, w_ref, out_ref, rows, near, far, wts):
    step = pl.program_id(0)
    vblk = table_ref.shape[1]

    @pl.when(step == 0)
    def _():
        tap = [w_ref[k] for k in range(5)]
        wts[...] = jnp.concatenate([tap[2], tap[0], tap[3], tap[1], jnp.zeros_like(tap[4]), tap[4]], axis=0)

    @pl.when(step < vblocks)
    def _():
        def project(i, _):
            at = pl.multiple_of(i * CHUNK, LANES)
            base = pl.multiple_of(step * vblk + at, LANES)
            part = lax.dot_general(
                table_ref[:, pl.ds(at, CHUNK)], wts[...], (((0,), (1,)), ((), ())),
                preferred_element_type=jnp.float32,
            )
            for col in range(3):
                rows[col, pl.ds(base, CHUNK), :] = part[:, col * LANES:(col + 1) * LANES]
            return 0

        lax.fori_loop(0, vblk // CHUNK, project, 0, unroll=True)

    @pl.when(step == vblocks)
    def _():
        for col in range(3):
            rows[col, pl.ds(vocab, PAD), :] = jnp.zeros((PAD, LANES), jnp.float32)
        for side in range(2):
            near[side, pl.ds(0, PAD), :] = jnp.zeros((PAD, LANES), jnp.float32)
            far[side, pl.ds(PAD + steps_out, PAD), :] = jnp.zeros((PAD, LANES), jnp.float32)

    @pl.when(step >= vblocks)
    def _():
        lane = lax.broadcasted_iota(jnp.int32, (steps_out, LANES), 1)
        for pair in range(group // 2):
            for side in range(2):
                rec = (step - vblocks) * group + pair * 2 + side
                live = live_ref[rec]
                tiles = (live + (UNROLL - 1)) // UNROLL

                def clear(i, _):
                    at = pl.ds(pl.multiple_of(PAD + i * UNROLL, UNROLL), UNROLL)
                    near[side, at, :] = jnp.zeros((UNROLL, LANES), jnp.float32)
                    far[side, at, :] = jnp.zeros((UNROLL, LANES), jnp.float32)
                    return 0

                lax.fori_loop(tiles, steps_out // UNROLL, clear, 0)

                def fetch(i, _):
                    start = rec * (2 * steps_out) + i * (2 * UNROLL)
                    for u in range(UNROLL):
                        even = ids_ref[start + 2 * u]
                        odd = ids_ref[start + 2 * u + 1]
                        at = pl.ds(PAD + i * UNROLL + u, 1)
                        near[side, at, :] = rows[0, pl.ds(even, 1), :] + rows[1, pl.ds(odd, 1), :]
                        far[side, at, :] = rows[2, pl.ds(even, 1), :]
                    return 0

                lax.fori_loop(0, tiles, fetch, 0)
            own0 = near[0, pl.ds(PAD, steps_out), :]
            own1 = near[1, pl.ds(PAD, steps_out), :]
            edge0 = near[0, pl.ds(PAD - 1, steps_out), :] + far[0, pl.ds(PAD + 1, steps_out), :]
            edge1 = near[1, pl.ds(PAD - 1, steps_out), :] + far[1, pl.ds(PAD + 1, steps_out), :]
            first = own0 + pltpu.roll(edge0, LANES // 2, 1)
            second = pltpu.roll(own1, LANES // 2, 1) + edge1
            out_ref[pair] = jnp.where(lane < LANES // 2, first, second)


def right_pairs(ids, live, table, weights, steps_out):
    vocab = table.shape[1]
    chans = table.shape[0]
    recipes = live.shape[0]
    vblk = 5 * CHUNK
    vblocks = vocab // vblk
    group = 8
    return pl.pallas_call(
        functools.partial(right_kernel, vocab, vblocks, group, steps_out),
        grid_spec=pltpu.PrefetchScalarGridSpec(
            num_scalar_prefetch=2,
            grid=(vblocks + recipes // group,),
            in_specs=[
                pl.BlockSpec((chans, vblk), lambda s, *_: (0, jnp.minimum(s, vblocks - 1))),
                pl.BlockSpec(weights.shape, lambda s, *_: (0, 0, 0)),
            ],
            out_specs=pl.BlockSpec(
                (group // 2, steps_out, LANES), lambda s, *_: (jnp.maximum(s - vblocks, 0), 0, 0)
            ),
            scratch_shapes=[
                pltpu.VMEM((3, vocab + PAD, LANES), jnp.float32),
                pltpu.VMEM((2, steps_out + 2 * PAD, LANES), jnp.float32),
                pltpu.VMEM((2, steps_out + 2 * PAD, LANES), jnp.float32),
                pltpu.VMEM((3 * LANES, chans), jnp.bfloat16),
            ],
        ),
        out_shape=jax.ShapeDtypeStruct((recipes // 2, steps_out, LANES), jnp.float32),
        compiler_params=pltpu.CompilerParams(vmem_limit_bytes=60 * 1024 * 1024),
        cost_estimate=pl.CostEstimate(
            flops=2 * vocab * chans * 3 * LANES, bytes_accessed=200 * 1024 * 1024, transcendentals=0
        ),
    )(ids, live, table, weights)


TILE = 128
GROUP = 4
BUFS = 4


def fused_kernel(
    dp_count, tok_ref, lens, table_hbm, cot_hbm, pa_ref, w_ref, out_ref,
    rows, tbuf, cbuf, lown, lgive, lgot, xout, xin, lfull, evens, odds, operand, tok2, wt, near, far, give, got, rsum,
    xs, xall, gs, gin, dg, dgin, fs, fin, ds, dfin, ids,
    cot_sem, tab_sem, ids_sem, s1_send, s1_recv, s2_send, s2_recv, s3_send, s3_recv, raw_send, raw_recv,
    x_send, x_recv, g_send, g_recv, d_send, d_recv, f_send, f_recv, df_send, df_recv,
):
    f32, bf16 = jnp.float32, jnp.bfloat16
    me = lax.axis_index("tensor")
    blk = lax.axis_index("dp")
    core = me % 2
    sib = me + 1 - 2 * core
    across = (me + 2) % 4
    mesh_ids = pl.DeviceIdType.MESH
    recs, chans, steps = cbuf.shape
    vblk = tbuf.shape[2]
    chunks = table_hbm.shape[1] // vblk
    groups = recs // GROUP
    seq = 2 * steps
    vocab = table_hbm.shape[1]
    width = pa_ref.shape[0]
    feats = width * width

    def remote(src, dst, send, recv, where):
        return pltpu.make_async_remote_copy(
            src_ref=src, dst_ref=dst, send_sem=send, recv_sem=recv, device_id=where, device_id_type=mesh_ids
        )

    def cot_copy(i):
        at = pl.ds(i * GROUP, GROUP)
        return pltpu.make_async_copy(cot_hbm.at[at], cbuf.at[at], cot_sem.at[i])

    def tab_copy(i):
        at = pl.ds(pl.multiple_of(i * vblk, TILE), vblk)
        return pltpu.make_async_copy(table_hbm.at[:, at], tbuf.at[i % BUFS], tab_sem.at[i % BUFS])

    def ids_copy(rec, k):
        return pltpu.make_async_copy(tok2.at[rec], ids.at[k], ids_sem.at[k])

    barrier = pltpu.get_barrier_semaphore()
    for i in range(groups):
        cot_copy(i).start()
    for off in range(1, 4):
        pl.semaphore_signal(barrier, inc=1, device_id={"tensor": (me + off) % 4}, device_id_type=mesh_ids)
    for off in range(1, dp_count):
        pl.semaphore_signal(barrier, inc=1, device_id={"dp": (blk + off) % dp_count}, device_id_type=mesh_ids)
    for i in range(BUFS):
        tab_copy(i).start()
    spot = lax.broadcasted_iota(jnp.int32, (1, seq), 1)
    for rec in range(recs):
        tok2[rec:rec + 1, :] = jnp.where(spot < lens[rec], tok_ref[rec:rec + 1, :] * 2, 2 * vocab)
    for k in range(GROUP):
        ids_copy(k, k).start()
    pl.semaphore_wait(barrier, 3 + dp_count - 1)

    def s1(i):
        return remote(lgive.at[i], lgot.at[i], s1_send.at[i], s1_recv.at[i], {"tensor": sib})

    def s2(i):
        return remote(xout.at[i], xin.at[i], s2_send.at[i], s2_recv.at[i], {"tensor": across})

    def s3(i):
        here = lfull.at[2 * i + core]
        return remote(here, here, s3_send.at[i], s3_recv.at[i], {"tensor": sib})

    def s3_in(i):
        there = lfull.at[2 * i + 1 - core]
        return remote(there, there, s3_send.at[i], s3_recv.at[i], {"tensor": sib})

    lane = lax.broadcasted_iota(jnp.int32, (width, steps), 1)

    for side, pairs in enumerate((((2, 0), (None, 4)), ((3, 1), (None, None)))):
        for col, halves in enumerate(pairs):
            block = [jnp.zeros((width, chans), bf16) if tap is None else w_ref[tap] for tap in halves]
            wt[side * chans:(side + 1) * chans, col * TILE:(col + 1) * TILE] = jnp.concatenate(block, axis=0).T
    near[...] = jnp.zeros(near.shape, f32)
    far[...] = jnp.zeros(far.shape, f32)
    rows[pl.ds(2 * vocab, 8), :] = jnp.zeros((8, TILE), f32)

    def left_step(i, _):
        cot_copy(i).wait()
        for dst, pair in ((lgive, 2 * i + 1 - core), (lown, 2 * i + core)):
            for s in range(2):
                rec = 2 * pair + s
                part = jnp.dot(pa_ref[...], cbuf[rec], preferred_element_type=f32)
                dst[i, s * width:(s + 1) * width, :] = jnp.where(2 * lane < lens[rec], part, 0.0)
        s1(i).start()
        return 0

    lax.fori_loop(0, groups, left_step, 0)

    def chip_step(i, _):
        s1(i).wait_recv()
        both = lown[i] + lgot[i]
        lown[i] = both
        xout[i] = both.astype(bf16)
        s2(i).start()
        return 0

    lax.fori_loop(0, groups, chip_step, 0)

    def turn(i, _):
        tab_copy(i).wait()
        slot = i % BUFS
        for j in range(vblk // TILE):
            base = pl.multiple_of(2 * (i * vblk + j * TILE), 2 * TILE)
            for h in range(2):
                part = tbuf[slot, h * TILE:(h + 1) * TILE, j * TILE:(j + 1) * TILE]
                rows[pl.ds(base + h, TILE, stride=2), :] = part.T.astype(f32)

        @pl.when(i + BUFS < chunks)
        def _():
            tab_copy(i + BUFS).start()

        return 0

    lax.fori_loop(0, chunks, turn, 0)

    def finish_left(i):
        s2(i).wait_recv()
        lfull[2 * i + core] = lown[i] + xin[i].astype(f32)
        s3(i).start()

    finish_left(0)

    def gather(k):
        for t in range(steps):
            evens[k, 2 * t:2 * t + 2, :] = rows[pl.ds(ids[k, 2 * t], 2), :]
            odds[k, 2 * t:2 * t + 2, :] = rows[pl.ds(ids[k, 2 * t + 1], 2), :]

    upper = lax.broadcasted_iota(jnp.int32, (steps, TILE), 1) >= TILE // 2
    upper_rows = lax.broadcasted_iota(jnp.int32, (8, TILE), 1) >= TILE // 2

    def project(g):
        for k in range(GROUP):
            for n, buf in enumerate((evens, odds)):
                for h in range(2):
                    col = (2 * n + h) * TILE
                    operand[k * steps:(k + 1) * steps, col:col + TILE] = buf[k, pl.ds(h, steps, stride=2), :].astype(bf16)
        taps = jnp.dot(operand[...], wt[...], preferred_element_type=f32)
        for k in range(GROUP):
            near[k, pl.ds(PAD, steps), :] = taps[k * steps:(k + 1) * steps, :TILE]
            far[k, pl.ds(PAD, steps), :] = taps[k * steps:(k + 1) * steps, TILE:]
        for k in range(GROUP):
            edge = near[k, pl.ds(PAD - 1, steps), :] + far[k, pl.ds(PAD + 1, steps), :]
            mixed = jnp.where(upper, edge, near[k, pl.ds(PAD, steps), :])
            right = mixed + pltpu.roll(mixed, TILE // 2, 1)
            high = right.astype(bf16).astype(f32)
            right = jnp.where(upper, right - high, high).astype(bf16)
            left = lfull[2 * g + k // 2, (k % 2) * width:(k % 2 + 1) * width, :]
            left_high = left.astype(bf16)
            left = jnp.concatenate([left_high, (left - left_high.astype(f32)).astype(bf16)], axis=0)
            raw = jnp.dot(left, right, preferred_element_type=f32)
            raw = raw[:width] + raw[width:]
            raw = raw + pltpu.roll(raw, TILE // 2, 1)
            for j in range(4):
                lo = 16 * j
                give[j, g * GROUP + k] = jnp.where(upper_rows, raw[lo + 8:lo + 16], raw[lo:lo + 8])

    def raw_copy(g, off):
        peer = (me + off) % 4
        at = pl.ds(g * GROUP, GROUP)
        return remote(
            give.at[peer, at], got.at[off - 1, at], raw_send.at[off - 1, g], raw_recv.at[off - 1, g], {"tensor": peer}
        )

    def group_step(g, _):
        @pl.when(g < groups - 1)
        def _():
            finish_left(g + 1)

        for k in range(GROUP):
            ids_copy(g * GROUP + k, k).wait()
            gather(k)

            @pl.when(g < groups - 1)
            def _():
                ids_copy((g + 1) * GROUP + k, k).start()

        s3_in(g).wait_recv()
        project(g)
        for off in range(1, 4):
            raw_copy(g, off).start()
        return 0

    lax.fori_loop(0, groups, group_step, 0)
    for g in range(groups):
        for off in range(1, 4):
            raw_copy(g, off).wait_recv()
    raw = (give[me] + got[0]) + (got[1] + got[2])
    rsum[...] = raw.reshape(recs * 8, TILE)
    for p in range(dp_count):
        xs[p] = rsum[pl.ds(p, recs, stride=8), :]
    xall[blk] = xs[blk]

    def x_copy(off):
        peer = (blk + off) % dp_count
        return remote(xs.at[peer], xall.at[blk], x_send.at[off - 1], x_recv.at[off - 1], {"dp": peer})

    offs = range(1, dp_count)
    for off in offs:
        x_copy(off).start()
    for off in offs:
        x_copy(off).wait_recv()
    every = xall[...].reshape(dp_count * recs, TILE)
    high = every.astype(bf16)
    low = (every - high.astype(f32)).astype(bf16)
    gram = lax.dot_general(
        jnp.concatenate([high, high, low], axis=1), jnp.concatenate([high, low, high], axis=1),
        (((1,), (1,)), ((), ())), preferred_element_type=f32,
    ).astype(bf16)
    for d in range(dp_count):
        gs[d] = gram[d * recs:(d + 1) * recs]
    count = dp_count * recs
    row_id = lax.broadcasted_iota(jnp.int32, (count, count), 0)
    col_id = lax.broadcasted_iota(jnp.int32, (count, count), 1)
    dg[...] = jnp.sum(jnp.where(row_id == col_id, gram.astype(f32), 0.0), axis=0, keepdims=True)

    def g_copy(off):
        peer = (blk + off) % dp_count
        return remote(gs.at[peer], gin.at[off - 1], g_send.at[off - 1], g_recv.at[off - 1], {"dp": peer})

    def d_copy(off):
        peer = (blk + off) % dp_count
        return remote(dg, dgin.at[off - 1], d_send.at[off - 1], d_recv.at[off - 1], {"dp": peer})

    for off in offs:
        g_copy(off).start()
        d_copy(off).start()
    mine = gs[blk].astype(f32)
    squares = dg[...]
    for off in offs:
        g_copy(off).wait_recv()
        d_copy(off).wait_recv()
        mine = mine + gin[off - 1].astype(f32)
        squares = squares + dgin[off - 1]
    out_rows = recs // 4
    for j in range(4):
        fs[j] = mine[j * out_rows:(j + 1) * out_rows]
    ds[...] = squares

    def f_copy(off):
        peer = (me + off) % 4
        return remote(fs.at[peer], fin.at[off - 1], f_send.at[off - 1], f_recv.at[off - 1], {"tensor": peer})

    def df_copy(off):
        return remote(ds, dfin.at[off - 1], df_send.at[off - 1], df_recv.at[off - 1], {"tensor": (me + off) % 4})

    for off in range(1, 4):
        f_copy(off).start()
        df_copy(off).start()
    total = fs[me]
    for off in range(1, 4):
        f_copy(off).wait_recv()
        df_copy(off).wait_recv()
        total = total + fin[off - 1]
        squares = squares + dfin[off - 1]
    scale = lax.rsqrt(squares * (1.0 / feats) + 1e-06)
    own_row = lax.broadcasted_iota(jnp.int32, (out_rows, count), 0) + (blk * recs + me * out_rows)
    own_col = lax.broadcasted_iota(jnp.int32, (out_rows, count), 1)
    row_scale = jnp.sum(jnp.where(own_row == own_col, scale, 0.0), axis=1, keepdims=True)
    out_ref[...] = total * scale * row_scale

    def sent(i, _):
        s1(i).wait_send()
        s2(i).wait_send()
        s3(i).wait_send()
        for off in range(1, 4):
            raw_copy(i, off).wait_send()
        return 0

    lax.fori_loop(0, groups, sent, 0)
    for off in offs:
        x_copy(off).wait_send()
        g_copy(off).wait_send()
        d_copy(off).wait_send()
    for off in range(1, 4):
        f_copy(off).wait_send()
        df_copy(off).wait_send()


def fused(ids, lengths, table, cotangent, proj_a, weights, dp_count):
    recs, chans, steps = cotangent.shape
    width = proj_a.shape[0]
    vocab = table.shape[1]
    groups = recs // GROUP
    count = dp_count * recs
    f32, bf16 = jnp.float32, jnp.bfloat16
    dma = pltpu.SemaphoreType.DMA
    hbm = pl.BlockSpec(memory_space=pl.ANY)
    vmem = pl.BlockSpec(memory_space=pltpu.VMEM)
    smem = pl.BlockSpec(memory_space=pltpu.SMEM)
    tokens = pltpu.VMEM((GROUP, 2 * steps, TILE), f32)
    padded = pltpu.VMEM((GROUP, steps + 2 * PAD, TILE), f32)
    lefts = pltpu.VMEM((groups, 2 * width, steps), f32)
    lefts_half = pltpu.VMEM((groups, 2 * width, steps), bf16)
    others = dp_count - 1
    return pl.pallas_call(
        functools.partial(fused_kernel, dp_count),
        out_shape=jax.ShapeDtypeStruct((recs // 4, count), f32),
        in_specs=[vmem, smem, hbm, hbm, vmem, vmem],
        out_specs=vmem,
        scratch_shapes=[
            pltpu.VMEM((2 * vocab + 8, TILE), f32),
            pltpu.VMEM((BUFS, chans, vocab // 10), bf16),
            pltpu.VMEM((recs, chans, steps), bf16),
            lefts, lefts, lefts, lefts_half, lefts_half,
            pltpu.VMEM((2 * groups, 2 * width, steps), f32),
            tokens, tokens,
            pltpu.VMEM((GROUP * steps, 4 * TILE), bf16),
            pltpu.VMEM((recs, 2 * steps), jnp.int32),
            pltpu.VMEM((2 * chans, 2 * TILE), bf16),
            padded, padded,
            pltpu.VMEM((4, recs, 8, TILE), f32),
            pltpu.VMEM((3, recs, 8, TILE), f32),
            pltpu.VMEM((recs * 8, TILE), f32),
            pltpu.VMEM((dp_count, recs, TILE), f32),
            pltpu.VMEM((dp_count, recs, TILE), f32),
            pltpu.VMEM((dp_count, recs, count), bf16),
            pltpu.VMEM((others, recs, count), bf16),
            pltpu.VMEM((1, count), f32),
            pltpu.VMEM((others, 1, count), f32),
            pltpu.VMEM((4, recs // 4, count), f32),
            pltpu.VMEM((3, recs // 4, count), f32),
            pltpu.VMEM((1, count), f32),
            pltpu.VMEM((3, 1, count), f32),
            pltpu.SMEM((GROUP, 2 * steps), jnp.int32),
            dma((groups,)), dma((BUFS,)), dma((GROUP,)),
            dma((groups,)), dma((groups,)), dma((groups,)), dma((groups,)), dma((groups,)), dma((groups,)),
            dma((3, groups)), dma((3, groups)),
            dma((others,)), dma((others,)), dma((others,)), dma((others,)), dma((others,)), dma((others,)),
            dma((3,)), dma((3,)), dma((3,)), dma((3,)),
        ],
        compiler_params=pltpu.CompilerParams(
            collective_id=0, has_side_effects=True, vmem_limit_bytes=56 * 1024 * 1024
        ),
        cost_estimate=pl.CostEstimate(flops=6 * 10**9, bytes_accessed=20 * 2**20, transcendentals=0),
    )(ids, lengths, table, cotangent, proj_a, weights)


def left_part_of(lengths, cotangent, proj_a):
    steps_out = cotangent.shape[2]
    outpos = 2 * jnp.arange(steps_out, dtype=jnp.int32)
    tkeep = outpos[None, :] < lengths[:, None]
    masked = jnp.where(tkeep[:, None, :], cotangent, jnp.zeros((), cotangent.dtype))
    return jnp.einsum("nct,ca->nat", masked, proj_a, preferred_element_type=jnp.float32)


def local(token_ids, lengths, table, cotangent, proj_a, proj_b):
    recipes_here, seqlen = token_ids.shape
    chans, width = proj_a.shape
    vocab = table.shape[1]
    steps_out = seqlen // 2
    total_feats = width * width
    if lax.axis_size("tensor") == 4 and lax.axis_size("dp") == 8:
        raw = fused(token_ids, lengths, table, cotangent, proj_a.T, jnp.transpose(proj_b, (1, 2, 0)), 8)
        return raw * (1.0 / total_feats)
    left_part = left_part_of(lengths, cotangent, proj_a)

    pos = jnp.arange(seqlen, dtype=jnp.int32)
    ids = jnp.where(pos[None, :] < lengths[:, None], token_ids, vocab).reshape(-1)
    live = (lengths + 1) // 2
    weights = jnp.transpose(proj_b, (1, 2, 0))
    left_own = lax.psum_scatter(left_part, "tensor", scatter_dimension=0, tiled=True)
    right_part = right_pairs(ids, live, table, weights, steps_out)
    right_own = lax.psum_scatter(right_part, "tensor", scatter_dimension=0, tiled=True)
    mine = right_own.shape[0] * 2
    left_two = left_own.reshape(mine // 2, 2, width, steps_out)
    raw = jnp.stack(
        [
            jnp.einsum(
                "nat,ntb->nab", left_two[:, side], right_own[:, :, side * width:(side + 1) * width],
                precision=lax.Precision.HIGHEST,
            )
            for side in range(2)
        ],
        axis=1,
    ).reshape(mine, total_feats)
    scale = lax.rsqrt(jnp.mean(raw * raw, axis=1) + 1e-06)
    unit = (raw * scale[:, None]).astype(jnp.bfloat16)
    every = lax.all_gather(unit, ("dp", "tensor"), axis=0, tiled=True)
    terms = lax.dot_general(
        unit, every, (((1,), (1,)), ((), ())), preferred_element_type=jnp.float32
    )
    return terms * (1.0 / total_feats)


def solution(mesh):
    placed = (
        P("dp", None),
        P("dp"),
        P("tensor", None),
        P("dp", "tensor", None),
        P("tensor", None),
        P("tensor", None, None),
    )
    return jax.shard_map(
        local, mesh=mesh, in_specs=placed, out_specs=P(("dp", "tensor"), None), check_vma=False
    )
```

```python
import functools

import jax
import jax.numpy as jnp
from jax import lax
from jax.experimental import pallas as pl
from jax.experimental.pallas import tpu as pltpu
from jax.sharding import PartitionSpec as P

LANES = 128
UNROLL = 32
PAD = 32
CHUNK = 640


def right_kernel(vocab, vblocks, group, steps_out, ids_ref, live_ref, table_ref, w_ref, out_ref, rows, near, far, wts):
    step = pl.program_id(0)
    vblk = table_ref.shape[1]

    @pl.when(step == 0)
    def _():
        tap = [w_ref[k] for k in range(5)]
        wts[...] = jnp.concatenate([tap[2], tap[0], tap[3], tap[1], jnp.zeros_like(tap[4]), tap[4]], axis=0)

    @pl.when(step < vblocks)
    def _():
        def project(i, _):
            at = pl.multiple_of(i * CHUNK, LANES)
            base = pl.multiple_of(step * vblk + at, LANES)
            part = lax.dot_general(
                table_ref[:, pl.ds(at, CHUNK)], wts[...], (((0,), (1,)), ((), ())),
                preferred_element_type=jnp.float32,
            )
            for col in range(3):
                rows[col, pl.ds(base, CHUNK), :] = part[:, col * LANES:(col + 1) * LANES]
            return 0

        lax.fori_loop(0, vblk // CHUNK, project, 0, unroll=True)

    @pl.when(step == vblocks)
    def _():
        for col in range(3):
            rows[col, pl.ds(vocab, PAD), :] = jnp.zeros((PAD, LANES), jnp.float32)
        for side in range(2):
            near[side, pl.ds(0, PAD), :] = jnp.zeros((PAD, LANES), jnp.float32)
            far[side, pl.ds(PAD + steps_out, PAD), :] = jnp.zeros((PAD, LANES), jnp.float32)

    @pl.when(step >= vblocks)
    def _():
        lane = lax.broadcasted_iota(jnp.int32, (steps_out, LANES), 1)
        for pair in range(group // 2):
            for side in range(2):
                rec = (step - vblocks) * group + pair * 2 + side
                live = live_ref[rec]
                tiles = (live + (UNROLL - 1)) // UNROLL

                def clear(i, _):
                    at = pl.ds(pl.multiple_of(PAD + i * UNROLL, UNROLL), UNROLL)
                    near[side, at, :] = jnp.zeros((UNROLL, LANES), jnp.float32)
                    far[side, at, :] = jnp.zeros((UNROLL, LANES), jnp.float32)
                    return 0

                lax.fori_loop(tiles, steps_out // UNROLL, clear, 0)

                def fetch(i, _):
                    start = rec * (2 * steps_out) + i * (2 * UNROLL)
                    for u in range(UNROLL):
                        even = ids_ref[start + 2 * u]
                        odd = ids_ref[start + 2 * u + 1]
                        at = pl.ds(PAD + i * UNROLL + u, 1)
                        near[side, at, :] = rows[0, pl.ds(even, 1), :] + rows[1, pl.ds(odd, 1), :]
                        far[side, at, :] = rows[2, pl.ds(even, 1), :]
                    return 0

                lax.fori_loop(0, tiles, fetch, 0)
            own0 = near[0, pl.ds(PAD, steps_out), :]
            own1 = near[1, pl.ds(PAD, steps_out), :]
            edge0 = near[0, pl.ds(PAD - 1, steps_out), :] + far[0, pl.ds(PAD + 1, steps_out), :]
            edge1 = near[1, pl.ds(PAD - 1, steps_out), :] + far[1, pl.ds(PAD + 1, steps_out), :]
            first = own0 + pltpu.roll(edge0, LANES // 2, 1)
            second = pltpu.roll(own1, LANES // 2, 1) + edge1
            out_ref[pair] = jnp.where(lane < LANES // 2, first, second)


def right_pairs(ids, live, table, weights, steps_out):
    vocab = table.shape[1]
    chans = table.shape[0]
    recipes = live.shape[0]
    vblk = 5 * CHUNK
    vblocks = vocab // vblk
    group = 8
    return pl.pallas_call(
        functools.partial(right_kernel, vocab, vblocks, group, steps_out),
        grid_spec=pltpu.PrefetchScalarGridSpec(
            num_scalar_prefetch=2,
            grid=(vblocks + recipes // group,),
            in_specs=[
                pl.BlockSpec((chans, vblk), lambda s, *_: (0, jnp.minimum(s, vblocks - 1))),
                pl.BlockSpec(weights.shape, lambda s, *_: (0, 0, 0)),
            ],
            out_specs=pl.BlockSpec(
                (group // 2, steps_out, LANES), lambda s, *_: (jnp.maximum(s - vblocks, 0), 0, 0)
            ),
            scratch_shapes=[
                pltpu.VMEM((3, vocab + PAD, LANES), jnp.float32),
                pltpu.VMEM((2, steps_out + 2 * PAD, LANES), jnp.float32),
                pltpu.VMEM((2, steps_out + 2 * PAD, LANES), jnp.float32),
                pltpu.VMEM((3 * LANES, chans), jnp.bfloat16),
            ],
        ),
        out_shape=jax.ShapeDtypeStruct((recipes // 2, steps_out, LANES), jnp.float32),
        compiler_params=pltpu.CompilerParams(vmem_limit_bytes=60 * 1024 * 1024),
        cost_estimate=pl.CostEstimate(
            flops=2 * vocab * chans * 3 * LANES, bytes_accessed=200 * 1024 * 1024, transcendentals=0
        ),
    )(ids, live, table, weights)


TILE = 128
GROUP = 4
BUFS = 4


def fused_kernel(
    dp_count, tok_ref, lens, table_hbm, cot_hbm, pa_ref, w_ref, out_ref,
    rows, tbuf, cbuf, lown, lgive, lgot, xout, xin, lfull, evens, odds, operand, tok2, wt, near, far, give, got, rsum,
    xs, xall, gs, gin, dg, dgin, fs, fin, ds, dfin, ids,
    cot_sem, tab_sem, ids_sem, s1_send, s1_recv, s2_send, s2_recv, s3_send, s3_recv, raw_send, raw_recv,
    x_send, x_recv, g_send, g_recv, d_send, d_recv, f_send, f_recv, df_send, df_recv,
):
    f32, bf16 = jnp.float32, jnp.bfloat16
    me = lax.axis_index("tensor")
    blk = lax.axis_index("dp")
    core = me % 2
    sib = me + 1 - 2 * core
    across = (me + 2) % 4
    mesh_ids = pl.DeviceIdType.MESH
    recs, chans, steps = cbuf.shape
    vblk = tbuf.shape[2]
    chunks = table_hbm.shape[1] // vblk
    groups = recs // GROUP
    seq = 2 * steps
    vocab = table_hbm.shape[1]
    width = pa_ref.shape[0]
    feats = width * width

    def remote(src, dst, send, recv, where):
        return pltpu.make_async_remote_copy(
            src_ref=src, dst_ref=dst, send_sem=send, recv_sem=recv, device_id=where, device_id_type=mesh_ids
        )

    def cot_copy(i):
        at = pl.ds(i * GROUP, GROUP)
        return pltpu.make_async_copy(cot_hbm.at[at], cbuf.at[at], cot_sem.at[i])

    def tab_copy(i):
        at = pl.ds(pl.multiple_of(i * vblk, TILE), vblk)
        return pltpu.make_async_copy(table_hbm.at[:, at], tbuf.at[i % BUFS], tab_sem.at[i % BUFS])

    def ids_copy(rec, k):
        return pltpu.make_async_copy(tok2.at[rec], ids.at[k], ids_sem.at[k])

    barrier = pltpu.get_barrier_semaphore()
    for i in range(BUFS):
        cot_copy(i).start()
        tab_copy(i).start()
    for i in range(BUFS, groups):
        cot_copy(i).start()
    for off in range(1, 4):
        pl.semaphore_signal(barrier, inc=1, device_id={"tensor": (me + off) % 4}, device_id_type=mesh_ids)
    for off in range(1, dp_count):
        pl.semaphore_signal(barrier, inc=1, device_id={"dp": (blk + off) % dp_count}, device_id_type=mesh_ids)
    spot = lax.broadcasted_iota(jnp.int32, (1, seq), 1)
    for rec in range(recs):
        tok2[rec:rec + 1, :] = jnp.where(spot < lens[rec], tok_ref[rec:rec + 1, :] * 2, 2 * vocab)
    for k in range(GROUP):
        ids_copy(k, k).start()

    def s1(i):
        return remote(lgive.at[i], lgot.at[i], s1_send.at[i], s1_recv.at[i], {"tensor": sib})

    def s2(i):
        return remote(xout.at[i], xin.at[i], s2_send.at[i], s2_recv.at[i], {"tensor": across})

    def s3(i):
        here = lfull.at[2 * i + core]
        return remote(here, here, s3_send.at[i], s3_recv.at[i], {"tensor": sib})

    def s3_in(i):
        there = lfull.at[2 * i + 1 - core]
        return remote(there, there, s3_send.at[i], s3_recv.at[i], {"tensor": sib})

    lane = lax.broadcasted_iota(jnp.int32, (width, steps), 1)

    for side, pairs in enumerate((((2, 0), (None, 4)), ((3, 1), (None, None)))):
        for col, halves in enumerate(pairs):
            block = [jnp.zeros((width, chans), bf16) if tap is None else w_ref[tap] for tap in halves]
            wt[side * chans:(side + 1) * chans, col * TILE:(col + 1) * TILE] = jnp.concatenate(block, axis=0).T
    near[...] = jnp.zeros(near.shape, f32)
    far[...] = jnp.zeros(far.shape, f32)
    rows[pl.ds(2 * vocab, 8), :] = jnp.zeros((8, TILE), f32)

    def left_step(i):
        cot_copy(i).wait()
        for dst, pair in ((lgive, 2 * i + 1 - core), (lown, 2 * i + core)):
            for s in range(2):
                rec = 2 * pair + s
                part = jnp.dot(pa_ref[...], cbuf[rec], preferred_element_type=f32)
                dst[i, s * width:(s + 1) * width, :] = jnp.where(2 * lane < lens[rec], part, 0.0)
        s1(i).start()

    def chip_step(i):
        s1(i).wait_recv()
        both = lown[i] + lgot[i]
        lown[i] = both
        xout[i] = both.astype(bf16)
        s2(i).start()

    def turn(i):
        tab_copy(i).wait()
        slot = i % BUFS
        for j in range(vblk // TILE):
            base = pl.multiple_of(2 * (i * vblk + j * TILE), 2 * TILE)
            for h in range(2):
                part = tbuf[slot, h * TILE:(h + 1) * TILE, j * TILE:(j + 1) * TILE]
                rows[pl.ds(base + h, TILE, stride=2), :] = part.T.astype(f32)

        @pl.when(i + BUFS < chunks)
        def _():
            tab_copy(i + BUFS).start()

    pl.semaphore_wait(barrier, 3 + dp_count - 1)

    def early_step(i, _):
        @pl.when(i < groups)
        def _():
            left_step(i)

        turn(i)

        @pl.when((i > 0) & (i <= groups))
        def _():
            chip_step(i - 1)

        return 0

    lax.fori_loop(0, chunks, early_step, 0)

    def finish_left(i):
        s2(i).wait_recv()
        lfull[2 * i + core] = lown[i] + xin[i].astype(f32)
        s3(i).start()

    finish_left(0)

    def gather(k):
        for t in range(steps):
            evens[k, 2 * t:2 * t + 2, :] = rows[pl.ds(ids[k, 2 * t], 2), :]
            odds[k, 2 * t:2 * t + 2, :] = rows[pl.ds(ids[k, 2 * t + 1], 2), :]

    upper = lax.broadcasted_iota(jnp.int32, (steps, TILE), 1) >= TILE // 2
    upper_rows = lax.broadcasted_iota(jnp.int32, (8, TILE), 1) >= TILE // 2

    def project(g):
        for k in range(GROUP):
            for n, buf in enumerate((evens, odds)):
                for h in range(2):
                    col = (2 * n + h) * TILE
                    operand[k * steps:(k + 1) * steps, col:col + TILE] = buf[k, pl.ds(h, steps, stride=2), :].astype(bf16)
        taps = jnp.dot(operand[...], wt[...], preferred_element_type=f32)
        for k in range(GROUP):
            near[k, pl.ds(PAD, steps), :] = taps[k * steps:(k + 1) * steps, :TILE]
            far[k, pl.ds(PAD, steps), :] = taps[k * steps:(k + 1) * steps, TILE:]
        for k in range(GROUP):
            edge = near[k, pl.ds(PAD - 1, steps), :] + far[k, pl.ds(PAD + 1, steps), :]
            mixed = jnp.where(upper, edge, near[k, pl.ds(PAD, steps), :])
            right = mixed + pltpu.roll(mixed, TILE // 2, 1)
            high = right.astype(bf16).astype(f32)
            right = jnp.where(upper, right - high, high).astype(bf16)
            left = lfull[2 * g + k // 2, (k % 2) * width:(k % 2 + 1) * width, :]
            left_high = left.astype(bf16)
            left = jnp.concatenate([left_high, (left - left_high.astype(f32)).astype(bf16)], axis=0)
            raw = jnp.dot(left, right, preferred_element_type=f32)
            raw = raw[:width] + raw[width:]
            raw = raw + pltpu.roll(raw, TILE // 2, 1)
            for j in range(4):
                lo = 16 * j
                give[j, g * GROUP + k] = jnp.where(upper_rows, raw[lo + 8:lo + 16], raw[lo:lo + 8])

    def raw_copy(g, off):
        peer = (me + off) % 4
        at = pl.ds(g * GROUP, GROUP)
        return remote(
            give.at[peer, at], got.at[off - 1, at], raw_send.at[off - 1, g], raw_recv.at[off - 1, g], {"tensor": peer}
        )

    offs = range(1, dp_count)

    def x_copy(c, off):
        peer = (blk + off) % dp_count
        at = pl.ds(pl.multiple_of(c * 8, 8), 8)
        return remote(
            xs.at[peer, at], xall.at[blk, at], x_send.at[off - 1, c], x_recv.at[off - 1, c], {"dp": peer}
        )

    def ship(c):
        for g in (2 * c, 2 * c + 1):
            for off in range(1, 4):
                raw_copy(g, off).wait_recv()
        at = pl.ds(pl.multiple_of(c * 8, 8), 8)
        base = pl.multiple_of(c * 64, 64)
        raw = (give[me, at] + got[0, at]) + (got[1, at] + got[2, at])
        rsum[pl.ds(base, 64), :] = raw.reshape(64, TILE)
        for p in range(dp_count):
            xs[p, at, :] = rsum[pl.ds(base + p, 8, stride=8), :]
        xall[blk, at, :] = xs[blk, at, :]
        for off in offs:
            x_copy(c, off).start()

    def group_step(g, _):
        @pl.when(g < groups - 1)
        def _():
            finish_left(g + 1)

        for k in range(GROUP):
            ids_copy(g * GROUP + k, k).wait()
            gather(k)

            @pl.when(g < groups - 1)
            def _():
                ids_copy((g + 1) * GROUP + k, k).start()

        s3_in(g).wait_recv()
        project(g)
        for off in range(1, 4):
            raw_copy(g, off).start()
        return 0

    lax.fori_loop(0, groups, group_step, 0)
    parts = recs // 8
    for c in range(parts):
        ship(c)
    for c in range(parts):
        for off in offs:
            x_copy(c, off).wait_recv()
    every = xall[...].reshape(dp_count * recs, TILE)
    high = every.astype(bf16)
    low = (every - high.astype(f32)).astype(bf16)
    gram = lax.dot_general(
        jnp.concatenate([high, high, low], axis=1), jnp.concatenate([high, low, high], axis=1),
        (((1,), (1,)), ((), ())), preferred_element_type=f32,
    )
    out_rows = recs // 4
    for j in range(4):
        starts = [d * recs + j * out_rows for d in range(dp_count)]
        gs[j] = jnp.concatenate([gram[at:at + out_rows] for at in starts], axis=0).astype(bf16)
    count = dp_count * recs
    row_id = lax.broadcasted_iota(jnp.int32, (count, count), 0)
    col_id = lax.broadcasted_iota(jnp.int32, (count, count), 1)
    rounded = gram.astype(bf16).astype(f32)
    dg[...] = jnp.sum(jnp.where(row_id == col_id, rounded, 0.0), axis=0, keepdims=True)

    def g_copy(off):
        peer = (me + off) % 4
        return remote(gs.at[peer], gin.at[off - 1], g_send.at[off - 1], g_recv.at[off - 1], {"tensor": peer})

    def d_copy(off):
        return remote(dg, dgin.at[off - 1], d_send.at[off - 1], d_recv.at[off - 1], {"tensor": (me + off) % 4})

    for off in range(1, 4):
        g_copy(off).start()
        d_copy(off).start()
    mine = gs[me].astype(f32)
    squares = dg[...]
    for off in range(1, 4):
        g_copy(off).wait_recv()
        d_copy(off).wait_recv()
        mine = mine + gin[off - 1].astype(f32)
        squares = squares + dgin[off - 1]
    for d in range(dp_count):
        fs[d] = mine[d * out_rows:(d + 1) * out_rows]
    ds[...] = squares

    def f_copy(off):
        peer = (blk + off) % dp_count
        return remote(fs.at[peer], fin.at[off - 1], f_send.at[off - 1], f_recv.at[off - 1], {"dp": peer})

    def df_copy(off):
        return remote(
            ds, dfin.at[off - 1], df_send.at[off - 1], df_recv.at[off - 1], {"dp": (blk + off) % dp_count}
        )

    for off in offs:
        f_copy(off).start()
        df_copy(off).start()
    total = fs[blk]
    for off in offs:
        f_copy(off).wait_recv()
        df_copy(off).wait_recv()
        total = total + fin[off - 1]
        squares = squares + dfin[off - 1]
    scale = lax.rsqrt(squares * (1.0 / feats) + 1e-06)
    own_row = lax.broadcasted_iota(jnp.int32, (out_rows, count), 0) + (blk * recs + me * out_rows)
    own_col = lax.broadcasted_iota(jnp.int32, (out_rows, count), 1)
    row_scale = jnp.sum(jnp.where(own_row == own_col, scale, 0.0), axis=1, keepdims=True)
    out_ref[...] = total * scale * row_scale

    def sent(i, _):
        s1(i).wait_send()
        s2(i).wait_send()
        s3(i).wait_send()
        for off in range(1, 4):
            raw_copy(i, off).wait_send()
        return 0

    lax.fori_loop(0, groups, sent, 0)
    for off in offs:
        for c in range(parts):
            x_copy(c, off).wait_send()
        f_copy(off).wait_send()
        df_copy(off).wait_send()
    for off in range(1, 4):
        g_copy(off).wait_send()
        d_copy(off).wait_send()


def fused(ids, lengths, table, cotangent, proj_a, weights, dp_count):
    recs, chans, steps = cotangent.shape
    width = proj_a.shape[0]
    vocab = table.shape[1]
    groups = recs // GROUP
    count = dp_count * recs
    f32, bf16 = jnp.float32, jnp.bfloat16
    dma = pltpu.SemaphoreType.DMA
    hbm = pl.BlockSpec(memory_space=pl.ANY)
    vmem = pl.BlockSpec(memory_space=pltpu.VMEM)
    smem = pl.BlockSpec(memory_space=pltpu.SMEM)
    tokens = pltpu.VMEM((GROUP, 2 * steps, TILE), f32)
    padded = pltpu.VMEM((GROUP, steps + 2 * PAD, TILE), f32)
    lefts = pltpu.VMEM((groups, 2 * width, steps), f32)
    lefts_half = pltpu.VMEM((groups, 2 * width, steps), bf16)
    others = dp_count - 1
    return pl.pallas_call(
        functools.partial(fused_kernel, dp_count),
        out_shape=jax.ShapeDtypeStruct((recs // 4, count), f32),
        in_specs=[vmem, smem, hbm, hbm, vmem, vmem],
        out_specs=vmem,
        scratch_shapes=[
            pltpu.VMEM((2 * vocab + 8, TILE), f32),
            pltpu.VMEM((BUFS, chans, vocab // 10), bf16),
            pltpu.VMEM((recs, chans, steps), bf16),
            lefts, lefts, lefts, lefts_half, lefts_half,
            pltpu.VMEM((2 * groups, 2 * width, steps), f32),
            tokens, tokens,
            pltpu.VMEM((GROUP * steps, 4 * TILE), bf16),
            pltpu.VMEM((recs, 2 * steps), jnp.int32),
            pltpu.VMEM((2 * chans, 2 * TILE), bf16),
            padded, padded,
            pltpu.VMEM((4, recs, 8, TILE), f32),
            pltpu.VMEM((3, recs, 8, TILE), f32),
            pltpu.VMEM((recs * 8, TILE), f32),
            pltpu.VMEM((dp_count, recs, TILE), f32),
            pltpu.VMEM((dp_count, recs, TILE), f32),
            pltpu.VMEM((4, count // 4, count), bf16),
            pltpu.VMEM((3, count // 4, count), bf16),
            pltpu.VMEM((1, count), f32),
            pltpu.VMEM((3, 1, count), f32),
            pltpu.VMEM((dp_count, recs // 4, count), f32),
            pltpu.VMEM((others, recs // 4, count), f32),
            pltpu.VMEM((1, count), f32),
            pltpu.VMEM((others, 1, count), f32),
            pltpu.SMEM((GROUP, 2 * steps), jnp.int32),
            dma((groups,)), dma((BUFS,)), dma((GROUP,)),
            dma((groups,)), dma((groups,)), dma((groups,)), dma((groups,)), dma((groups,)), dma((groups,)),
            dma((3, groups)), dma((3, groups)),
            dma((others, recs // 8)), dma((others, recs // 8)), dma((3,)), dma((3,)), dma((3,)), dma((3,)),
            dma((others,)), dma((others,)), dma((others,)), dma((others,)),
        ],
        compiler_params=pltpu.CompilerParams(
            collective_id=0, has_side_effects=True, vmem_limit_bytes=56 * 1024 * 1024
        ),
        cost_estimate=pl.CostEstimate(flops=6 * 10**9, bytes_accessed=20 * 2**20, transcendentals=0),
    )(ids, lengths, table, cotangent, proj_a, weights)


def left_part_of(lengths, cotangent, proj_a):
    steps_out = cotangent.shape[2]
    outpos = 2 * jnp.arange(steps_out, dtype=jnp.int32)
    tkeep = outpos[None, :] < lengths[:, None]
    masked = jnp.where(tkeep[:, None, :], cotangent, jnp.zeros((), cotangent.dtype))
    return jnp.einsum("nct,ca->nat", masked, proj_a, preferred_element_type=jnp.float32)


def local(token_ids, lengths, table, cotangent, proj_a, proj_b):
    recipes_here, seqlen = token_ids.shape
    chans, width = proj_a.shape
    vocab = table.shape[1]
    steps_out = seqlen // 2
    total_feats = width * width
    if lax.axis_size("tensor") == 4 and lax.axis_size("dp") == 8:
        raw = fused(token_ids, lengths, table, cotangent, proj_a.T, jnp.transpose(proj_b, (1, 2, 0)), 8)
        return raw * (1.0 / total_feats)
    left_part = left_part_of(lengths, cotangent, proj_a)

    pos = jnp.arange(seqlen, dtype=jnp.int32)
    ids = jnp.where(pos[None, :] < lengths[:, None], token_ids, vocab).reshape(-1)
    live = (lengths + 1) // 2
    weights = jnp.transpose(proj_b, (1, 2, 0))
    left_own = lax.psum_scatter(left_part, "tensor", scatter_dimension=0, tiled=True)
    right_part = right_pairs(ids, live, table, weights, steps_out)
    right_own = lax.psum_scatter(right_part, "tensor", scatter_dimension=0, tiled=True)
    mine = right_own.shape[0] * 2
    left_two = left_own.reshape(mine // 2, 2, width, steps_out)
    raw = jnp.stack(
        [
            jnp.einsum(
                "nat,ntb->nab", left_two[:, side], right_own[:, :, side * width:(side + 1) * width],
                precision=lax.Precision.HIGHEST,
            )
            for side in range(2)
        ],
        axis=1,
    ).reshape(mine, total_feats)
    scale = lax.rsqrt(jnp.mean(raw * raw, axis=1) + 1e-06)
    unit = (raw * scale[:, None]).astype(jnp.bfloat16)
    every = lax.all_gather(unit, ("dp", "tensor"), axis=0, tiled=True)
    terms = lax.dot_general(
        unit, every, (((1,), (1,)), ((), ())), preferred_element_type=jnp.float32
    )
    return terms * (1.0 / total_feats)


def solution(mesh):
    placed = (
        P("dp", None),
        P("dp"),
        P("tensor", None),
        P("dp", "tensor", None),
        P("tensor", None),
        P("tensor", None, None),
    )
    return jax.shard_map(
        local, mesh=mesh, in_specs=placed, out_specs=P(("dp", "tensor"), None), check_vma=False
    )
```

```python
import functools

import jax
import jax.numpy as jnp
from jax import lax
from jax.experimental import pallas as pl
from jax.experimental.pallas import tpu as pltpu
from jax.sharding import PartitionSpec as P

LANES = 128
UNROLL = 32
PAD = 32
CHUNK = 640


def right_kernel(vocab, vblocks, group, steps_out, ids_ref, live_ref, table_ref, w_ref, out_ref, rows, near, far, wts):
    step = pl.program_id(0)
    vblk = table_ref.shape[1]

    @pl.when(step == 0)
    def _():
        tap = [w_ref[k] for k in range(5)]
        wts[...] = jnp.concatenate([tap[2], tap[0], tap[3], tap[1], jnp.zeros_like(tap[4]), tap[4]], axis=0)

    @pl.when(step < vblocks)
    def _():
        def project(i, _):
            at = pl.multiple_of(i * CHUNK, LANES)
            base = pl.multiple_of(step * vblk + at, LANES)
            part = lax.dot_general(
                table_ref[:, pl.ds(at, CHUNK)], wts[...], (((0,), (1,)), ((), ())),
                preferred_element_type=jnp.float32,
            )
            for col in range(3):
                rows[col, pl.ds(base, CHUNK), :] = part[:, col * LANES:(col + 1) * LANES]
            return 0

        lax.fori_loop(0, vblk // CHUNK, project, 0, unroll=True)

    @pl.when(step == vblocks)
    def _():
        for col in range(3):
            rows[col, pl.ds(vocab, PAD), :] = jnp.zeros((PAD, LANES), jnp.float32)
        for side in range(2):
            near[side, pl.ds(0, PAD), :] = jnp.zeros((PAD, LANES), jnp.float32)
            far[side, pl.ds(PAD + steps_out, PAD), :] = jnp.zeros((PAD, LANES), jnp.float32)

    @pl.when(step >= vblocks)
    def _():
        lane = lax.broadcasted_iota(jnp.int32, (steps_out, LANES), 1)
        for pair in range(group // 2):
            for side in range(2):
                rec = (step - vblocks) * group + pair * 2 + side
                live = live_ref[rec]
                tiles = (live + (UNROLL - 1)) // UNROLL

                def clear(i, _):
                    at = pl.ds(pl.multiple_of(PAD + i * UNROLL, UNROLL), UNROLL)
                    near[side, at, :] = jnp.zeros((UNROLL, LANES), jnp.float32)
                    far[side, at, :] = jnp.zeros((UNROLL, LANES), jnp.float32)
                    return 0

                lax.fori_loop(tiles, steps_out // UNROLL, clear, 0)

                def fetch(i, _):
                    start = rec * (2 * steps_out) + i * (2 * UNROLL)
                    for u in range(UNROLL):
                        even = ids_ref[start + 2 * u]
                        odd = ids_ref[start + 2 * u + 1]
                        at = pl.ds(PAD + i * UNROLL + u, 1)
                        near[side, at, :] = rows[0, pl.ds(even, 1), :] + rows[1, pl.ds(odd, 1), :]
                        far[side, at, :] = rows[2, pl.ds(even, 1), :]
                    return 0

                lax.fori_loop(0, tiles, fetch, 0)
            own0 = near[0, pl.ds(PAD, steps_out), :]
            own1 = near[1, pl.ds(PAD, steps_out), :]
            edge0 = near[0, pl.ds(PAD - 1, steps_out), :] + far[0, pl.ds(PAD + 1, steps_out), :]
            edge1 = near[1, pl.ds(PAD - 1, steps_out), :] + far[1, pl.ds(PAD + 1, steps_out), :]
            first = own0 + pltpu.roll(edge0, LANES // 2, 1)
            second = pltpu.roll(own1, LANES // 2, 1) + edge1
            out_ref[pair] = jnp.where(lane < LANES // 2, first, second)


def right_pairs(ids, live, table, weights, steps_out):
    vocab = table.shape[1]
    chans = table.shape[0]
    recipes = live.shape[0]
    vblk = 5 * CHUNK
    vblocks = vocab // vblk
    group = 8
    return pl.pallas_call(
        functools.partial(right_kernel, vocab, vblocks, group, steps_out),
        grid_spec=pltpu.PrefetchScalarGridSpec(
            num_scalar_prefetch=2,
            grid=(vblocks + recipes // group,),
            in_specs=[
                pl.BlockSpec((chans, vblk), lambda s, *_: (0, jnp.minimum(s, vblocks - 1))),
                pl.BlockSpec(weights.shape, lambda s, *_: (0, 0, 0)),
            ],
            out_specs=pl.BlockSpec(
                (group // 2, steps_out, LANES), lambda s, *_: (jnp.maximum(s - vblocks, 0), 0, 0)
            ),
            scratch_shapes=[
                pltpu.VMEM((3, vocab + PAD, LANES), jnp.float32),
                pltpu.VMEM((2, steps_out + 2 * PAD, LANES), jnp.float32),
                pltpu.VMEM((2, steps_out + 2 * PAD, LANES), jnp.float32),
                pltpu.VMEM((3 * LANES, chans), jnp.bfloat16),
            ],
        ),
        out_shape=jax.ShapeDtypeStruct((recipes // 2, steps_out, LANES), jnp.float32),
        compiler_params=pltpu.CompilerParams(vmem_limit_bytes=60 * 1024 * 1024),
        cost_estimate=pl.CostEstimate(
            flops=2 * vocab * chans * 3 * LANES, bytes_accessed=200 * 1024 * 1024, transcendentals=0
        ),
    )(ids, live, table, weights)


TILE = 128
GROUP = 4
BUFS = 4


def fused_kernel(
    dp_count, tok_ref, lens, table_hbm, cot_hbm, pa_ref, w_ref, out_ref,
    rows, tbuf, cbuf, lown, lgive, lgot, xout, xin, lfull, evens, odds, operand, tok2, wt, near, far, give, got, rsum,
    xs, xall, gs, gin, dg, dgin, fs, fin, ds, dfin, ids,
    cot_sem, tab_sem, ids_sem, s1_send, s1_recv, s2_send, s2_recv, s3_send, s3_recv, raw_send, raw_recv,
    x_send, x_recv, g_send, g_recv, d_send, d_recv, f_send, f_recv, df_send, df_recv,
):
    f32, bf16 = jnp.float32, jnp.bfloat16
    me = lax.axis_index("tensor")
    blk = lax.axis_index("dp")
    core = me % 2
    sib = me + 1 - 2 * core
    across = (me + 2) % 4
    mesh_ids = pl.DeviceIdType.MESH
    recs, chans, steps = cbuf.shape
    vblk = tbuf.shape[2]
    chunks = table_hbm.shape[1] // vblk
    groups = recs // GROUP
    seq = 2 * steps
    vocab = table_hbm.shape[1]
    width = pa_ref.shape[0]
    feats = width * width

    def remote(src, dst, send, recv, where):
        return pltpu.make_async_remote_copy(
            src_ref=src, dst_ref=dst, send_sem=send, recv_sem=recv, device_id=where, device_id_type=mesh_ids
        )

    def cot_copy(i):
        at = pl.ds(i * GROUP, GROUP)
        return pltpu.make_async_copy(cot_hbm.at[at], cbuf.at[at], cot_sem.at[i])

    def tab_copy(i):
        at = pl.ds(pl.multiple_of(i * vblk, TILE), vblk)
        return pltpu.make_async_copy(table_hbm.at[:, at], tbuf.at[i % BUFS], tab_sem.at[i % BUFS])

    def ids_copy(rec, k):
        return pltpu.make_async_copy(tok2.at[rec], ids.at[k], ids_sem.at[k])

    barrier = pltpu.get_barrier_semaphore()
    for i in range(BUFS):
        cot_copy(i).start()
        tab_copy(i).start()
    for i in range(BUFS, groups):
        cot_copy(i).start()
    for off in range(1, 4):
        pl.semaphore_signal(barrier, inc=1, device_id={"tensor": (me + off) % 4}, device_id_type=mesh_ids)
    for off in range(1, dp_count):
        pl.semaphore_signal(barrier, inc=1, device_id={"dp": (blk + off) % dp_count}, device_id_type=mesh_ids)
    spot = lax.broadcasted_iota(jnp.int32, (1, seq), 1)
    for rec in range(recs):
        tok2[rec:rec + 1, :] = jnp.where(spot < lens[rec], tok_ref[rec:rec + 1, :] * 2, 2 * vocab)
    for k in range(GROUP):
        ids_copy(k, k).start()

    def s1(i):
        return remote(lgive.at[i], lgot.at[i], s1_send.at[i], s1_recv.at[i], {"tensor": sib})

    def s2(i):
        return remote(xout.at[i], xin.at[i], s2_send.at[i], s2_recv.at[i], {"tensor": across})

    def s3(i):
        here = lfull.at[2 * i + core]
        return remote(here, here, s3_send.at[i], s3_recv.at[i], {"tensor": sib})

    def s3_in(i):
        there = lfull.at[2 * i + 1 - core]
        return remote(there, there, s3_send.at[i], s3_recv.at[i], {"tensor": sib})

    lane = lax.broadcasted_iota(jnp.int32, (width, steps), 1)

    for side, pairs in enumerate((((2, 0), (None, 4)), ((3, 1), (None, None)))):
        for col, halves in enumerate(pairs):
            block = [jnp.zeros((width, chans), bf16) if tap is None else w_ref[tap] for tap in halves]
            wt[side * chans:(side + 1) * chans, col * TILE:(col + 1) * TILE] = jnp.concatenate(block, axis=0).T
    near[...] = jnp.zeros(near.shape, f32)
    far[...] = jnp.zeros(far.shape, f32)
    rows[pl.ds(2 * vocab, 8), :] = jnp.zeros((8, TILE), f32)

    def left_step(i):
        cot_copy(i).wait()
        for dst, pair in ((lgive, 2 * i + 1 - core), (lown, 2 * i + core)):
            for s in range(2):
                rec = 2 * pair + s
                part = jnp.dot(pa_ref[...], cbuf[rec], preferred_element_type=f32)
                dst[i, s * width:(s + 1) * width, :] = jnp.where(2 * lane < lens[rec], part, 0.0)
        s1(i).start()

    def chip_step(i):
        s1(i).wait_recv()
        both = lown[i] + lgot[i]
        lown[i] = both
        xout[i] = both.astype(bf16)
        s2(i).start()

    def turn(i):
        tab_copy(i).wait()
        slot = i % BUFS
        for j in range(vblk // TILE):
            base = pl.multiple_of(2 * (i * vblk + j * TILE), 2 * TILE)
            for h in range(2):
                part = tbuf[slot, h * TILE:(h + 1) * TILE, j * TILE:(j + 1) * TILE]
                rows[pl.ds(base + h, TILE, stride=2), :] = part.T.astype(f32)

        @pl.when(i + BUFS < chunks)
        def _():
            tab_copy(i + BUFS).start()

    pl.semaphore_wait(barrier, 3 + dp_count - 1)

    def each_left(i, _):
        left_step(i)
        return 0

    def each_chip(i, _):
        chip_step(i)
        return 0

    lax.fori_loop(0, groups, each_left, 0)

    def early_step(i, _):
        turn(i)

        @pl.when(i == 0)
        def _():
            lax.fori_loop(0, groups, each_chip, 0)

        return 0

    lax.fori_loop(0, chunks, early_step, 0)

    def finish_left(i):
        s2(i).wait_recv()
        lfull[2 * i + core] = lown[i] + xin[i].astype(f32)
        s3(i).start()

    finish_left(0)

    def gather(k):
        for t in range(steps):
            evens[k, 2 * t:2 * t + 2, :] = rows[pl.ds(ids[k, 2 * t], 2), :]
            odds[k, 2 * t:2 * t + 2, :] = rows[pl.ds(ids[k, 2 * t + 1], 2), :]

    upper = lax.broadcasted_iota(jnp.int32, (steps, TILE), 1) >= TILE // 2
    upper_rows = lax.broadcasted_iota(jnp.int32, (8, TILE), 1) >= TILE // 2

    def project(g):
        for k in range(GROUP):
            for n, buf in enumerate((evens, odds)):
                for h in range(2):
                    col = (2 * n + h) * TILE
                    operand[k * steps:(k + 1) * steps, col:col + TILE] = buf[k, pl.ds(h, steps, stride=2), :].astype(bf16)
        taps = jnp.dot(operand[...], wt[...], preferred_element_type=f32)
        for k in range(GROUP):
            near[k, pl.ds(PAD, steps), :] = taps[k * steps:(k + 1) * steps, :TILE]
            far[k, pl.ds(PAD, steps), :] = taps[k * steps:(k + 1) * steps, TILE:]
        for k in range(GROUP):
            edge = near[k, pl.ds(PAD - 1, steps), :] + far[k, pl.ds(PAD + 1, steps), :]
            mixed = jnp.where(upper, edge, near[k, pl.ds(PAD, steps), :])
            right = mixed + pltpu.roll(mixed, TILE // 2, 1)
            high = right.astype(bf16).astype(f32)
            right = jnp.where(upper, right - high, high).astype(bf16)
            left = lfull[2 * g + k // 2, (k % 2) * width:(k % 2 + 1) * width, :]
            left_high = left.astype(bf16)
            left = jnp.concatenate([left_high, (left - left_high.astype(f32)).astype(bf16)], axis=0)
            raw = jnp.dot(left, right, preferred_element_type=f32)
            raw = raw[:width] + raw[width:]
            raw = raw + pltpu.roll(raw, TILE // 2, 1)
            for j in range(4):
                lo = 16 * j
                give[j, g * GROUP + k] = jnp.where(upper_rows, raw[lo + 8:lo + 16], raw[lo:lo + 8])

    def raw_copy(g, off):
        peer = (me + off) % 4
        at = pl.ds(g * GROUP, GROUP)
        return remote(
            give.at[peer, at], got.at[off - 1, at], raw_send.at[off - 1, g], raw_recv.at[off - 1, g], {"tensor": peer}
        )

    offs = range(1, dp_count)

    def x_copy(c, off):
        peer = (blk + off) % dp_count
        at = pl.ds(pl.multiple_of(c * 8, 8), 8)
        return remote(
            xs.at[peer, at], xall.at[blk, at], x_send.at[off - 1, c], x_recv.at[off - 1, c], {"dp": peer}
        )

    def ship(c):
        for g in (2 * c, 2 * c + 1):
            for off in range(1, 4):
                raw_copy(g, off).wait_recv()
        at = pl.ds(pl.multiple_of(c * 8, 8), 8)
        base = pl.multiple_of(c * 64, 64)
        raw = (give[me, at] + got[0, at]) + (got[1, at] + got[2, at])
        rsum[pl.ds(base, 64), :] = raw.reshape(64, TILE)
        for p in range(dp_count):
            xs[p, at, :] = rsum[pl.ds(base + p, 8, stride=8), :]
        xall[blk, at, :] = xs[blk, at, :]
        for off in offs:
            x_copy(c, off).start()

    def group_step(g, _):
        for k in range(GROUP):
            ids_copy(g * GROUP + k, k).wait()
            gather(k)

            @pl.when(g < groups - 1)
            def _():
                ids_copy((g + 1) * GROUP + k, k).start()

        @pl.when(g < groups - 1)
        def _():
            finish_left(g + 1)

        s3_in(g).wait_recv()
        project(g)
        for off in range(1, 4):
            raw_copy(g, off).start()
        return 0

    lax.fori_loop(0, groups, group_step, 0)
    parts = recs // 8
    for c in range(parts):
        ship(c)
    for c in range(parts):
        for off in offs:
            x_copy(c, off).wait_recv()
    every = xall[...].reshape(dp_count * recs, TILE)
    high = every.astype(bf16)
    low = (every - high.astype(f32)).astype(bf16)
    gram = lax.dot_general(
        jnp.concatenate([high, high, low], axis=1), jnp.concatenate([high, low, high], axis=1),
        (((1,), (1,)), ((), ())), preferred_element_type=f32,
    )
    out_rows = recs // 4
    for j in range(4):
        starts = [d * recs + j * out_rows for d in range(dp_count)]
        gs[j] = jnp.concatenate([gram[at:at + out_rows] for at in starts], axis=0).astype(bf16)
    count = dp_count * recs
    row_id = lax.broadcasted_iota(jnp.int32, (count, count), 0)
    col_id = lax.broadcasted_iota(jnp.int32, (count, count), 1)
    rounded = gram.astype(bf16).astype(f32)
    dg[...] = jnp.sum(jnp.where(row_id == col_id, rounded, 0.0), axis=0, keepdims=True)

    def g_copy(off):
        peer = (me + off) % 4
        return remote(gs.at[peer], gin.at[off - 1], g_send.at[off - 1], g_recv.at[off - 1], {"tensor": peer})

    def d_copy(off):
        return remote(dg, dgin.at[off - 1], d_send.at[off - 1], d_recv.at[off - 1], {"tensor": (me + off) % 4})

    for off in range(1, 4):
        g_copy(off).start()
        d_copy(off).start()
    mine = gs[me].astype(f32)
    squares = dg[...]
    for off in range(1, 4):
        g_copy(off).wait_recv()
        d_copy(off).wait_recv()
        mine = mine + gin[off - 1].astype(f32)
        squares = squares + dgin[off - 1]
    for d in range(dp_count):
        fs[d] = mine[d * out_rows:(d + 1) * out_rows]
    ds[...] = squares

    def f_copy(off):
        peer = (blk + off) % dp_count
        return remote(fs.at[peer], fin.at[off - 1], f_send.at[off - 1], f_recv.at[off - 1], {"dp": peer})

    def df_copy(off):
        return remote(
            ds, dfin.at[off - 1], df_send.at[off - 1], df_recv.at[off - 1], {"dp": (blk + off) % dp_count}
        )

    for off in offs:
        f_copy(off).start()
        df_copy(off).start()
    total = fs[blk]
    for off in offs:
        f_copy(off).wait_recv()
        df_copy(off).wait_recv()
        total = total + fin[off - 1]
        squares = squares + dfin[off - 1]
    scale = lax.rsqrt(squares * (1.0 / feats) + 1e-06)
    own_row = lax.broadcasted_iota(jnp.int32, (out_rows, count), 0) + (blk * recs + me * out_rows)
    own_col = lax.broadcasted_iota(jnp.int32, (out_rows, count), 1)
    row_scale = jnp.sum(jnp.where(own_row == own_col, scale, 0.0), axis=1, keepdims=True)
    out_ref[...] = total * scale * row_scale

    def sent(i, _):
        s1(i).wait_send()
        s2(i).wait_send()
        s3(i).wait_send()
        for off in range(1, 4):
            raw_copy(i, off).wait_send()
        return 0

    lax.fori_loop(0, groups, sent, 0)
    for off in offs:
        for c in range(parts):
            x_copy(c, off).wait_send()
        f_copy(off).wait_send()
        df_copy(off).wait_send()
    for off in range(1, 4):
        g_copy(off).wait_send()
        d_copy(off).wait_send()


def fused(ids, lengths, table, cotangent, proj_a, weights, dp_count):
    recs, chans, steps = cotangent.shape
    width = proj_a.shape[0]
    vocab = table.shape[1]
    groups = recs // GROUP
    count = dp_count * recs
    f32, bf16 = jnp.float32, jnp.bfloat16
    dma = pltpu.SemaphoreType.DMA
    hbm = pl.BlockSpec(memory_space=pl.ANY)
    vmem = pl.BlockSpec(memory_space=pltpu.VMEM)
    smem = pl.BlockSpec(memory_space=pltpu.SMEM)
    tokens = pltpu.VMEM((GROUP, 2 * steps, TILE), f32)
    padded = pltpu.VMEM((GROUP, steps + 2 * PAD, TILE), f32)
    lefts = pltpu.VMEM((groups, 2 * width, steps), f32)
    lefts_half = pltpu.VMEM((groups, 2 * width, steps), bf16)
    others = dp_count - 1
    return pl.pallas_call(
        functools.partial(fused_kernel, dp_count),
        out_shape=pltpu.VMEM((recs // 4, count), f32),
        in_specs=[vmem, smem, hbm, hbm, vmem, vmem],
        out_specs=vmem,
        scratch_shapes=[
            pltpu.VMEM((2 * vocab + 8, TILE), f32),
            pltpu.VMEM((BUFS, chans, vocab // 10), bf16),
            pltpu.VMEM((recs, chans, steps), bf16),
            lefts, lefts, lefts, lefts_half, lefts_half,
            pltpu.VMEM((2 * groups, 2 * width, steps), f32),
            tokens, tokens,
            pltpu.VMEM((GROUP * steps, 4 * TILE), bf16),
            pltpu.VMEM((recs, 2 * steps), jnp.int32),
            pltpu.VMEM((2 * chans, 2 * TILE), bf16),
            padded, padded,
            pltpu.VMEM((4, recs, 8, TILE), f32),
            pltpu.VMEM((3, recs, 8, TILE), f32),
            pltpu.VMEM((recs * 8, TILE), f32),
            pltpu.VMEM((dp_count, recs, TILE), f32),
            pltpu.VMEM((dp_count, recs, TILE), f32),
            pltpu.VMEM((4, count // 4, count), bf16),
            pltpu.VMEM((3, count // 4, count), bf16),
            pltpu.VMEM((1, count), f32),
            pltpu.VMEM((3, 1, count), f32),
            pltpu.VMEM((dp_count, recs // 4, count), f32),
            pltpu.VMEM((others, recs // 4, count), f32),
            pltpu.VMEM((1, count), f32),
            pltpu.VMEM((others, 1, count), f32),
            pltpu.SMEM((GROUP, 2 * steps), jnp.int32),
            dma((groups,)), dma((BUFS,)), dma((GROUP,)),
            dma((groups,)), dma((groups,)), dma((groups,)), dma((groups,)), dma((groups,)), dma((groups,)),
            dma((3, groups)), dma((3, groups)),
            dma((others, recs // 8)), dma((others, recs // 8)), dma((3,)), dma((3,)), dma((3,)), dma((3,)),
            dma((others,)), dma((others,)), dma((others,)), dma((others,)),
        ],
        compiler_params=pltpu.CompilerParams(
            collective_id=0, has_side_effects=True, vmem_limit_bytes=56 * 1024 * 1024
        ),
        cost_estimate=pl.CostEstimate(flops=6 * 10**9, bytes_accessed=20 * 2**20, transcendentals=0),
    )(ids, lengths, table, cotangent, proj_a, weights)


def left_part_of(lengths, cotangent, proj_a):
    steps_out = cotangent.shape[2]
    outpos = 2 * jnp.arange(steps_out, dtype=jnp.int32)
    tkeep = outpos[None, :] < lengths[:, None]
    masked = jnp.where(tkeep[:, None, :], cotangent, jnp.zeros((), cotangent.dtype))
    return jnp.einsum("nct,ca->nat", masked, proj_a, preferred_element_type=jnp.float32)


def local(token_ids, lengths, table, cotangent, proj_a, proj_b):
    recipes_here, seqlen = token_ids.shape
    chans, width = proj_a.shape
    vocab = table.shape[1]
    steps_out = seqlen // 2
    total_feats = width * width
    if lax.axis_size("tensor") == 4 and lax.axis_size("dp") == 8:
        raw = fused(token_ids, lengths, table, cotangent, proj_a.T, jnp.transpose(proj_b, (1, 2, 0)), 8)
        return raw * (1.0 / total_feats)
    left_part = left_part_of(lengths, cotangent, proj_a)

    pos = jnp.arange(seqlen, dtype=jnp.int32)
    ids = jnp.where(pos[None, :] < lengths[:, None], token_ids, vocab).reshape(-1)
    live = (lengths + 1) // 2
    weights = jnp.transpose(proj_b, (1, 2, 0))
    left_own = lax.psum_scatter(left_part, "tensor", scatter_dimension=0, tiled=True)
    right_part = right_pairs(ids, live, table, weights, steps_out)
    right_own = lax.psum_scatter(right_part, "tensor", scatter_dimension=0, tiled=True)
    mine = right_own.shape[0] * 2
    left_two = left_own.reshape(mine // 2, 2, width, steps_out)
    raw = jnp.stack(
        [
            jnp.einsum(
                "nat,ntb->nab", left_two[:, side], right_own[:, :, side * width:(side + 1) * width],
                precision=lax.Precision.HIGHEST,
            )
            for side in range(2)
        ],
        axis=1,
    ).reshape(mine, total_feats)
    scale = lax.rsqrt(jnp.mean(raw * raw, axis=1) + 1e-06)
    unit = (raw * scale[:, None]).astype(jnp.bfloat16)
    every = lax.all_gather(unit, ("dp", "tensor"), axis=0, tiled=True)
    terms = lax.dot_general(
        unit, every, (((1,), (1,)), ((), ())), preferred_element_type=jnp.float32
    )
    return terms * (1.0 / total_feats)


def solution(mesh):
    placed = (
        P("dp", None),
        P("dp"),
        P("tensor", None),
        P("dp", "tensor", None),
        P("tensor", None),
        P("tensor", None, None),
    )
    return jax.shard_map(
        local, mesh=mesh, in_specs=placed, out_specs=P(("dp", "tensor"), None), check_vma=False
    )
```

```python
import functools

import jax
import jax.numpy as jnp
from jax import lax
from jax.experimental import pallas as pl
from jax.experimental.pallas import tpu as pltpu
from jax.sharding import PartitionSpec as P

LANES = 128
UNROLL = 32
PAD = 32
CHUNK = 640


def right_kernel(vocab, vblocks, group, steps_out, ids_ref, live_ref, table_ref, w_ref, out_ref, rows, near, far, wts):
    step = pl.program_id(0)
    vblk = table_ref.shape[1]

    @pl.when(step == 0)
    def _():
        tap = [w_ref[k] for k in range(5)]
        wts[...] = jnp.concatenate([tap[2], tap[0], tap[3], tap[1], jnp.zeros_like(tap[4]), tap[4]], axis=0)

    @pl.when(step < vblocks)
    def _():
        def project(i, _):
            at = pl.multiple_of(i * CHUNK, LANES)
            base = pl.multiple_of(step * vblk + at, LANES)
            part = lax.dot_general(
                table_ref[:, pl.ds(at, CHUNK)], wts[...], (((0,), (1,)), ((), ())),
                preferred_element_type=jnp.float32,
            )
            for col in range(3):
                rows[col, pl.ds(base, CHUNK), :] = part[:, col * LANES:(col + 1) * LANES]
            return 0

        lax.fori_loop(0, vblk // CHUNK, project, 0, unroll=True)

    @pl.when(step == vblocks)
    def _():
        for col in range(3):
            rows[col, pl.ds(vocab, PAD), :] = jnp.zeros((PAD, LANES), jnp.float32)
        for side in range(2):
            near[side, pl.ds(0, PAD), :] = jnp.zeros((PAD, LANES), jnp.float32)
            far[side, pl.ds(PAD + steps_out, PAD), :] = jnp.zeros((PAD, LANES), jnp.float32)

    @pl.when(step >= vblocks)
    def _():
        lane = lax.broadcasted_iota(jnp.int32, (steps_out, LANES), 1)
        for pair in range(group // 2):
            for side in range(2):
                rec = (step - vblocks) * group + pair * 2 + side
                live = live_ref[rec]
                tiles = (live + (UNROLL - 1)) // UNROLL

                def clear(i, _):
                    at = pl.ds(pl.multiple_of(PAD + i * UNROLL, UNROLL), UNROLL)
                    near[side, at, :] = jnp.zeros((UNROLL, LANES), jnp.float32)
                    far[side, at, :] = jnp.zeros((UNROLL, LANES), jnp.float32)
                    return 0

                lax.fori_loop(tiles, steps_out // UNROLL, clear, 0)

                def fetch(i, _):
                    start = rec * (2 * steps_out) + i * (2 * UNROLL)
                    for u in range(UNROLL):
                        even = ids_ref[start + 2 * u]
                        odd = ids_ref[start + 2 * u + 1]
                        at = pl.ds(PAD + i * UNROLL + u, 1)
                        near[side, at, :] = rows[0, pl.ds(even, 1), :] + rows[1, pl.ds(odd, 1), :]
                        far[side, at, :] = rows[2, pl.ds(even, 1), :]
                    return 0

                lax.fori_loop(0, tiles, fetch, 0)
            own0 = near[0, pl.ds(PAD, steps_out), :]
            own1 = near[1, pl.ds(PAD, steps_out), :]
            edge0 = near[0, pl.ds(PAD - 1, steps_out), :] + far[0, pl.ds(PAD + 1, steps_out), :]
            edge1 = near[1, pl.ds(PAD - 1, steps_out), :] + far[1, pl.ds(PAD + 1, steps_out), :]
            first = own0 + pltpu.roll(edge0, LANES // 2, 1)
            second = pltpu.roll(own1, LANES // 2, 1) + edge1
            out_ref[pair] = jnp.where(lane < LANES // 2, first, second)


def right_pairs(ids, live, table, weights, steps_out):
    vocab = table.shape[1]
    chans = table.shape[0]
    recipes = live.shape[0]
    vblk = 5 * CHUNK
    vblocks = vocab // vblk
    group = 8
    return pl.pallas_call(
        functools.partial(right_kernel, vocab, vblocks, group, steps_out),
        grid_spec=pltpu.PrefetchScalarGridSpec(
            num_scalar_prefetch=2,
            grid=(vblocks + recipes // group,),
            in_specs=[
                pl.BlockSpec((chans, vblk), lambda s, *_: (0, jnp.minimum(s, vblocks - 1))),
                pl.BlockSpec(weights.shape, lambda s, *_: (0, 0, 0)),
            ],
            out_specs=pl.BlockSpec(
                (group // 2, steps_out, LANES), lambda s, *_: (jnp.maximum(s - vblocks, 0), 0, 0)
            ),
            scratch_shapes=[
                pltpu.VMEM((3, vocab + PAD, LANES), jnp.float32),
                pltpu.VMEM((2, steps_out + 2 * PAD, LANES), jnp.float32),
                pltpu.VMEM((2, steps_out + 2 * PAD, LANES), jnp.float32),
                pltpu.VMEM((3 * LANES, chans), jnp.bfloat16),
            ],
        ),
        out_shape=jax.ShapeDtypeStruct((recipes // 2, steps_out, LANES), jnp.float32),
        compiler_params=pltpu.CompilerParams(vmem_limit_bytes=60 * 1024 * 1024),
        cost_estimate=pl.CostEstimate(
            flops=2 * vocab * chans * 3 * LANES, bytes_accessed=200 * 1024 * 1024, transcendentals=0
        ),
    )(ids, live, table, weights)


TILE = 128
GROUP = 4
BUFS = 4
EARLY = 1


def fused_kernel(
    dp_count, tok_ref, lens, table_hbm, cot_hbm, pa_ref, w_ref, out_ref,
    rows, tbuf, cbuf, lown, lgive, lgot, xout, xin, lfull, evens, odds, operand, tok2, wt, near, far, give, got, rsum,
    xs, xall, gs, gin, dg, dgin, fs, fin, ds, dfin, ids,
    cot_sem, tab_sem, ids_sem, s1_send, s1_recv, s2_send, s2_recv, s3_send, s3_recv, raw_send, raw_recv,
    x_send, x_recv, g_send, g_recv, d_send, d_recv, f_send, f_recv, df_send, df_recv,
):
    f32, bf16 = jnp.float32, jnp.bfloat16
    me = lax.axis_index("tensor")
    blk = lax.axis_index("dp")
    core = me % 2
    sib = me + 1 - 2 * core
    across = (me + 2) % 4
    mesh_ids = pl.DeviceIdType.MESH
    recs, chans, steps = cbuf.shape
    vblk = tbuf.shape[2]
    chunks = table_hbm.shape[1] // vblk
    groups = recs // GROUP
    seq = 2 * steps
    vocab = table_hbm.shape[1]
    width = pa_ref.shape[0]
    feats = width * width

    def remote(src, dst, send, recv, where):
        return pltpu.make_async_remote_copy(
            src_ref=src, dst_ref=dst, send_sem=send, recv_sem=recv, device_id=where, device_id_type=mesh_ids
        )

    def cot_copy(i):
        at = pl.ds(i * GROUP, GROUP)
        return pltpu.make_async_copy(cot_hbm.at[at], cbuf.at[at], cot_sem.at[i])

    def tab_copy(i):
        at = pl.ds(pl.multiple_of(i * vblk, TILE), vblk)
        return pltpu.make_async_copy(table_hbm.at[:, at], tbuf.at[i % BUFS], tab_sem.at[i % BUFS])

    def ids_copy(rec, k):
        return pltpu.make_async_copy(tok2.at[rec], ids.at[k], ids_sem.at[k])

    barrier = pltpu.get_barrier_semaphore()
    for i in range(BUFS):
        cot_copy(i).start()
        tab_copy(i).start()
    for i in range(BUFS, groups):
        cot_copy(i).start()
    for off in range(1, 4):
        pl.semaphore_signal(barrier, inc=1, device_id={"tensor": (me + off) % 4}, device_id_type=mesh_ids)
    for off in range(1, dp_count):
        pl.semaphore_signal(barrier, inc=1, device_id={"dp": (blk + off) % dp_count}, device_id_type=mesh_ids)
    spot = lax.broadcasted_iota(jnp.int32, (1, seq), 1)
    for rec in range(recs):
        tok2[rec:rec + 1, :] = jnp.where(spot < lens[rec], tok_ref[rec:rec + 1, :] * 2, 2 * vocab)
    for k in range(GROUP):
        ids_copy(k, k).start()

    def s1(i):
        return remote(lgive.at[i], lgot.at[i], s1_send.at[i], s1_recv.at[i], {"tensor": sib})

    def s2(i):
        return remote(xout.at[i], xin.at[i], s2_send.at[i], s2_recv.at[i], {"tensor": across})

    def s3(i):
        here = lfull.at[2 * i + core]
        return remote(here, here, s3_send.at[i], s3_recv.at[i], {"tensor": sib})

    def s3_in(i):
        there = lfull.at[2 * i + 1 - core]
        return remote(there, there, s3_send.at[i], s3_recv.at[i], {"tensor": sib})

    lane = lax.broadcasted_iota(jnp.int32, (width, steps), 1)

    for side, pairs in enumerate((((2, 0), (None, 4)), ((3, 1), (None, None)))):
        for col, halves in enumerate(pairs):
            block = [jnp.zeros((width, chans), bf16) if tap is None else w_ref[tap] for tap in halves]
            wt[side * chans:(side + 1) * chans, col * TILE:(col + 1) * TILE] = jnp.concatenate(block, axis=0).T
    near[...] = jnp.zeros(near.shape, f32)
    far[...] = jnp.zeros(far.shape, f32)
    rows[pl.ds(2 * vocab, 8), :] = jnp.zeros((8, TILE), f32)

    def left_step(i):
        cot_copy(i).wait()
        for dst, pair in ((lgive, 2 * i + 1 - core), (lown, 2 * i + core)):
            for s in range(2):
                rec = 2 * pair + s
                part = jnp.dot(pa_ref[...], cbuf[rec], preferred_element_type=f32)
                dst[i, s * width:(s + 1) * width, :] = jnp.where(2 * lane < lens[rec], part, 0.0)

    def chip_step(i):
        s1(i).wait_recv()
        both = lown[i] + lgot[i]
        lown[i] = both
        xout[i] = both.astype(bf16)
        s2(i).start()

    def turn(i):
        tab_copy(i).wait()
        slot = i % BUFS
        for j in range(vblk // TILE):
            base = pl.multiple_of(2 * (i * vblk + j * TILE), 2 * TILE)
            for h in range(2):
                part = tbuf[slot, h * TILE:(h + 1) * TILE, j * TILE:(j + 1) * TILE]
                rows[pl.ds(base + h, TILE, stride=2), :] = part.T.astype(f32)

        @pl.when(i + BUFS < chunks)
        def _():
            tab_copy(i + BUFS).start()


    def each(step):
        def body(i, _):
            step(i)
            return 0

        return body

    lax.fori_loop(0, groups, each(left_step), 0)
    lax.fori_loop(0, EARLY, each(turn), 0)
    pl.semaphore_wait(barrier, 3 + dp_count - 1)
    for i in range(groups):
        s1(i).start()
    lax.fori_loop(EARLY, EARLY + 2, each(turn), 0)
    lax.fori_loop(0, groups // 2, each(chip_step), 0)

    def late_turn(i):
        turn(i)

        @pl.when(i == EARLY + 2)
        def _():
            lax.fori_loop(groups // 2, groups, each(chip_step), 0)

    lax.fori_loop(EARLY + 2, chunks, each(late_turn), 0)

    def finish_left(i):
        s2(i).wait_recv()
        lfull[2 * i + core] = lown[i] + xin[i].astype(f32)
        s3(i).start()

    finish_left(0)

    def gather(k):
        for t in range(steps):
            evens[k, 2 * t:2 * t + 2, :] = rows[pl.ds(ids[k, 2 * t], 2), :]
            odds[k, 2 * t:2 * t + 2, :] = rows[pl.ds(ids[k, 2 * t + 1], 2), :]

    upper = lax.broadcasted_iota(jnp.int32, (steps, TILE), 1) >= TILE // 2
    upper_rows = lax.broadcasted_iota(jnp.int32, (8, TILE), 1) >= TILE // 2

    def project(g):
        for k in range(GROUP):
            for n, buf in enumerate((evens, odds)):
                for h in range(2):
                    col = (2 * n + h) * TILE
                    operand[k * steps:(k + 1) * steps, col:col + TILE] = buf[k, pl.ds(h, steps, stride=2), :].astype(bf16)
        from_even = jnp.dot(operand[:, :chans], wt[:chans], preferred_element_type=f32)
        from_odd = jnp.dot(operand[:, chans:], wt[chans:, :TILE], preferred_element_type=f32)
        for k in range(GROUP):
            at = slice(k * steps, (k + 1) * steps)
            near[k, pl.ds(PAD, steps), :] = from_even[at, :TILE] + from_odd[at]
            far[k, pl.ds(PAD, steps), :] = from_even[at, TILE:]
        for k in range(GROUP):
            edge = near[k, pl.ds(PAD - 1, steps), :] + far[k, pl.ds(PAD + 1, steps), :]
            mixed = jnp.where(upper, edge, near[k, pl.ds(PAD, steps), :])
            right = mixed + pltpu.roll(mixed, TILE // 2, 1)
            high = right.astype(bf16).astype(f32)
            right = jnp.where(upper, right - high, high).astype(bf16)
            left = lfull[2 * g + k // 2, (k % 2) * width:(k % 2 + 1) * width, :]
            left_high = left.astype(bf16)
            left = jnp.concatenate([left_high, (left - left_high.astype(f32)).astype(bf16)], axis=0)
            raw = jnp.dot(left, right, preferred_element_type=f32)
            raw = raw[:width] + raw[width:]
            raw = raw + pltpu.roll(raw, TILE // 2, 1)
            for j in range(4):
                lo = 16 * j
                give[j, g * GROUP + k] = jnp.where(upper_rows, raw[lo + 8:lo + 16], raw[lo:lo + 8])

    def raw_copy(g, off):
        peer = (me + off) % 4
        at = pl.ds(g * GROUP, GROUP)
        return remote(
            give.at[peer, at], got.at[off - 1, at], raw_send.at[off - 1, g], raw_recv.at[off - 1, g], {"tensor": peer}
        )

    offs = range(1, dp_count)

    def x_copy(c, off):
        peer = (blk + off) % dp_count
        at = pl.ds(pl.multiple_of(c * 8, 8), 8)
        return remote(
            xs.at[peer, at], xall.at[blk, at], x_send.at[off - 1, c], x_recv.at[off - 1, c], {"dp": peer}
        )

    def ship(c):
        for g in (2 * c, 2 * c + 1):
            for off in range(1, 4):
                raw_copy(g, off).wait_recv()
        at = pl.ds(pl.multiple_of(c * 8, 8), 8)
        base = pl.multiple_of(c * 64, 64)
        raw = (give[me, at] + got[0, at]) + (got[1, at] + got[2, at])
        rsum[pl.ds(base, 64), :] = raw.reshape(64, TILE)
        for p in range(dp_count):
            xs[p, at, :] = rsum[pl.ds(base + p, 8, stride=8), :]
        xall[blk, at, :] = xs[blk, at, :]
        for off in offs:
            x_copy(c, off).start()

    def group_step(g, _):
        for k in range(GROUP):
            ids_copy(g * GROUP + k, k).wait()
            gather(k)

            @pl.when(g < groups - 1)
            def _():
                ids_copy((g + 1) * GROUP + k, k).start()

        @pl.when(g < groups - 1)
        def _():
            finish_left(g + 1)

        s3_in(g).wait_recv()
        project(g)
        for off in range(1, 4):
            raw_copy(g, off).start()
        return 0

    lax.fori_loop(0, groups, group_step, 0)
    parts = recs // 8
    for c in range(parts):
        ship(c)
    for c in range(parts):
        for off in offs:
            x_copy(c, off).wait_recv()
    every = xall[...].reshape(dp_count * recs, TILE)
    high = every.astype(bf16)
    low = (every - high.astype(f32)).astype(bf16)
    gram = lax.dot_general(
        jnp.concatenate([high, high, low], axis=1), jnp.concatenate([high, low, high], axis=1),
        (((1,), (1,)), ((), ())), preferred_element_type=f32,
    )
    out_rows = recs // 4
    for j in range(4):
        starts = [d * recs + j * out_rows for d in range(dp_count)]
        gs[j] = jnp.concatenate([gram[at:at + out_rows] for at in starts], axis=0).astype(bf16)
    count = dp_count * recs
    row_id = lax.broadcasted_iota(jnp.int32, (count, count), 0)
    col_id = lax.broadcasted_iota(jnp.int32, (count, count), 1)
    rounded = gram.astype(bf16).astype(f32)
    dg[...] = jnp.sum(jnp.where(row_id == col_id, rounded, 0.0), axis=0, keepdims=True)

    def g_copy(off):
        peer = (me + off) % 4
        return remote(gs.at[peer], gin.at[off - 1], g_send.at[off - 1], g_recv.at[off - 1], {"tensor": peer})

    def d_copy(off):
        return remote(dg, dgin.at[off - 1], d_send.at[off - 1], d_recv.at[off - 1], {"tensor": (me + off) % 4})

    for off in range(1, 4):
        g_copy(off).start()
        d_copy(off).start()
    mine = gs[me].astype(f32)
    squares = dg[...]
    for off in range(1, 4):
        g_copy(off).wait_recv()
        d_copy(off).wait_recv()
        mine = mine + gin[off - 1].astype(f32)
        squares = squares + dgin[off - 1]
    for d in range(dp_count):
        fs[d] = mine[d * out_rows:(d + 1) * out_rows]
    ds[...] = squares

    def f_copy(off):
        peer = (blk + off) % dp_count
        return remote(fs.at[peer], fin.at[off - 1], f_send.at[off - 1], f_recv.at[off - 1], {"dp": peer})

    def df_copy(off):
        return remote(
            ds, dfin.at[off - 1], df_send.at[off - 1], df_recv.at[off - 1], {"dp": (blk + off) % dp_count}
        )

    for off in offs:
        f_copy(off).start()
        df_copy(off).start()
    total = fs[blk]
    for off in offs:
        f_copy(off).wait_recv()
        df_copy(off).wait_recv()
        total = total + fin[off - 1]
        squares = squares + dfin[off - 1]
    scale = lax.rsqrt(squares * (1.0 / feats) + 1e-06)
    own_row = lax.broadcasted_iota(jnp.int32, (out_rows, count), 0) + (blk * recs + me * out_rows)
    own_col = lax.broadcasted_iota(jnp.int32, (out_rows, count), 1)
    row_scale = jnp.sum(jnp.where(own_row == own_col, scale, 0.0), axis=1, keepdims=True)
    out_ref[...] = total * scale * row_scale

    def sent(i, _):
        s1(i).wait_send()
        s2(i).wait_send()
        s3(i).wait_send()
        for off in range(1, 4):
            raw_copy(i, off).wait_send()
        return 0

    lax.fori_loop(0, groups, sent, 0)
    for off in offs:
        for c in range(parts):
            x_copy(c, off).wait_send()
        f_copy(off).wait_send()
        df_copy(off).wait_send()
    for off in range(1, 4):
        g_copy(off).wait_send()
        d_copy(off).wait_send()


def fused(ids, lengths, table, cotangent, proj_a, weights, dp_count):
    recs, chans, steps = cotangent.shape
    width = proj_a.shape[0]
    vocab = table.shape[1]
    groups = recs // GROUP
    count = dp_count * recs
    f32, bf16 = jnp.float32, jnp.bfloat16
    dma = pltpu.SemaphoreType.DMA
    hbm = pl.BlockSpec(memory_space=pl.ANY)
    vmem = pl.BlockSpec(memory_space=pltpu.VMEM)
    smem = pl.BlockSpec(memory_space=pltpu.SMEM)
    tokens = pltpu.VMEM((GROUP, 2 * steps, TILE), f32)
    padded = pltpu.VMEM((GROUP, steps + 2 * PAD, TILE), f32)
    lefts = pltpu.VMEM((groups, 2 * width, steps), f32)
    lefts_half = pltpu.VMEM((groups, 2 * width, steps), bf16)
    others = dp_count - 1
    return pl.pallas_call(
        functools.partial(fused_kernel, dp_count),
        out_shape=pltpu.VMEM((recs // 4, count), f32),
        in_specs=[vmem, smem, hbm, hbm, vmem, vmem],
        out_specs=vmem,
        scratch_shapes=[
            pltpu.VMEM((2 * vocab + 8, TILE), f32),
            pltpu.VMEM((BUFS, chans, vocab // 10), bf16),
            pltpu.VMEM((recs, chans, steps), bf16),
            lefts, lefts, lefts, lefts_half, lefts_half,
            pltpu.VMEM((2 * groups, 2 * width, steps), f32),
            tokens, tokens,
            pltpu.VMEM((GROUP * steps, 4 * TILE), bf16),
            pltpu.VMEM((recs, 2 * steps), jnp.int32),
            pltpu.VMEM((2 * chans, 2 * TILE), bf16),
            padded, padded,
            pltpu.VMEM((4, recs, 8, TILE), f32),
            pltpu.VMEM((3, recs, 8, TILE), f32),
            pltpu.VMEM((recs * 8, TILE), f32),
            pltpu.VMEM((dp_count, recs, TILE), f32),
            pltpu.VMEM((dp_count, recs, TILE), f32),
            pltpu.VMEM((4, count // 4, count), bf16),
            pltpu.VMEM((3, count // 4, count), bf16),
            pltpu.VMEM((1, count), f32),
            pltpu.VMEM((3, 1, count), f32),
            pltpu.VMEM((dp_count, recs // 4, count), f32),
            pltpu.VMEM((others, recs // 4, count), f32),
            pltpu.VMEM((1, count), f32),
            pltpu.VMEM((others, 1, count), f32),
            pltpu.SMEM((GROUP, 2 * steps), jnp.int32),
            dma((groups,)), dma((BUFS,)), dma((GROUP,)),
            dma((groups,)), dma((groups,)), dma((groups,)), dma((groups,)), dma((groups,)), dma((groups,)),
            dma((3, groups)), dma((3, groups)),
            dma((others, recs // 8)), dma((others, recs // 8)), dma((3,)), dma((3,)), dma((3,)), dma((3,)),
            dma((others,)), dma((others,)), dma((others,)), dma((others,)),
        ],
        compiler_params=pltpu.CompilerParams(
            collective_id=0, has_side_effects=True, vmem_limit_bytes=56 * 1024 * 1024
        ),
        cost_estimate=pl.CostEstimate(flops=6 * 10**9, bytes_accessed=20 * 2**20, transcendentals=0),
    )(ids, lengths, table, cotangent, proj_a, weights)


def left_part_of(lengths, cotangent, proj_a):
    steps_out = cotangent.shape[2]
    outpos = 2 * jnp.arange(steps_out, dtype=jnp.int32)
    tkeep = outpos[None, :] < lengths[:, None]
    masked = jnp.where(tkeep[:, None, :], cotangent, jnp.zeros((), cotangent.dtype))
    return jnp.einsum("nct,ca->nat", masked, proj_a, preferred_element_type=jnp.float32)


def local(token_ids, lengths, table, cotangent, proj_a, proj_b):
    recipes_here, seqlen = token_ids.shape
    chans, width = proj_a.shape
    vocab = table.shape[1]
    steps_out = seqlen // 2
    total_feats = width * width
    if lax.axis_size("tensor") == 4 and lax.axis_size("dp") == 8:
        raw = fused(token_ids, lengths, table, cotangent, proj_a.T, jnp.transpose(proj_b, (1, 2, 0)), 8)
        return raw * (1.0 / total_feats)
    left_part = left_part_of(lengths, cotangent, proj_a)

    pos = jnp.arange(seqlen, dtype=jnp.int32)
    ids = jnp.where(pos[None, :] < lengths[:, None], token_ids, vocab).reshape(-1)
    live = (lengths + 1) // 2
    weights = jnp.transpose(proj_b, (1, 2, 0))
    left_own = lax.psum_scatter(left_part, "tensor", scatter_dimension=0, tiled=True)
    right_part = right_pairs(ids, live, table, weights, steps_out)
    right_own = lax.psum_scatter(right_part, "tensor", scatter_dimension=0, tiled=True)
    mine = right_own.shape[0] * 2
    left_two = left_own.reshape(mine // 2, 2, width, steps_out)
    raw = jnp.stack(
        [
            jnp.einsum(
                "nat,ntb->nab", left_two[:, side], right_own[:, :, side * width:(side + 1) * width],
                precision=lax.Precision.HIGHEST,
            )
            for side in range(2)
        ],
        axis=1,
    ).reshape(mine, total_feats)
    scale = lax.rsqrt(jnp.mean(raw * raw, axis=1) + 1e-06)
    unit = (raw * scale[:, None]).astype(jnp.bfloat16)
    every = lax.all_gather(unit, ("dp", "tensor"), axis=0, tiled=True)
    terms = lax.dot_general(
        unit, every, (((1,), (1,)), ((), ())), preferred_element_type=jnp.float32
    )
    return terms * (1.0 / total_feats)


def solution(mesh):
    placed = (
        P("dp", None),
        P("dp"),
        P("tensor", None),
        P("dp", "tensor", None),
        P("tensor", None),
        P("tensor", None, None),
    )
    return jax.shard_map(
        local, mesh=mesh, in_specs=placed, out_specs=P(("dp", "tensor"), None), check_vma=False
    )
```

```python
import functools

import jax
import jax.numpy as jnp
from jax import lax
from jax.experimental import pallas as pl
from jax.experimental.pallas import tpu as pltpu
from jax.sharding import PartitionSpec as P

LANES = 128
UNROLL = 32
PAD = 32
CHUNK = 640


def right_kernel(vocab, vblocks, group, steps_out, ids_ref, live_ref, table_ref, w_ref, out_ref, rows, near, far, wts):
    step = pl.program_id(0)
    vblk = table_ref.shape[1]

    @pl.when(step == 0)
    def _():
        tap = [w_ref[k] for k in range(5)]
        wts[...] = jnp.concatenate([tap[2], tap[0], tap[3], tap[1], jnp.zeros_like(tap[4]), tap[4]], axis=0)

    @pl.when(step < vblocks)
    def _():
        def project(i, _):
            at = pl.multiple_of(i * CHUNK, LANES)
            base = pl.multiple_of(step * vblk + at, LANES)
            part = lax.dot_general(
                table_ref[:, pl.ds(at, CHUNK)], wts[...], (((0,), (1,)), ((), ())),
                preferred_element_type=jnp.float32,
            )
            for col in range(3):
                rows[col, pl.ds(base, CHUNK), :] = part[:, col * LANES:(col + 1) * LANES]
            return 0

        lax.fori_loop(0, vblk // CHUNK, project, 0, unroll=True)

    @pl.when(step == vblocks)
    def _():
        for col in range(3):
            rows[col, pl.ds(vocab, PAD), :] = jnp.zeros((PAD, LANES), jnp.float32)
        for side in range(2):
            near[side, pl.ds(0, PAD), :] = jnp.zeros((PAD, LANES), jnp.float32)
            far[side, pl.ds(PAD + steps_out, PAD), :] = jnp.zeros((PAD, LANES), jnp.float32)

    @pl.when(step >= vblocks)
    def _():
        lane = lax.broadcasted_iota(jnp.int32, (steps_out, LANES), 1)
        for pair in range(group // 2):
            for side in range(2):
                rec = (step - vblocks) * group + pair * 2 + side
                live = live_ref[rec]
                tiles = (live + (UNROLL - 1)) // UNROLL

                def clear(i, _):
                    at = pl.ds(pl.multiple_of(PAD + i * UNROLL, UNROLL), UNROLL)
                    near[side, at, :] = jnp.zeros((UNROLL, LANES), jnp.float32)
                    far[side, at, :] = jnp.zeros((UNROLL, LANES), jnp.float32)
                    return 0

                lax.fori_loop(tiles, steps_out // UNROLL, clear, 0)

                def fetch(i, _):
                    start = rec * (2 * steps_out) + i * (2 * UNROLL)
                    for u in range(UNROLL):
                        even = ids_ref[start + 2 * u]
                        odd = ids_ref[start + 2 * u + 1]
                        at = pl.ds(PAD + i * UNROLL + u, 1)
                        near[side, at, :] = rows[0, pl.ds(even, 1), :] + rows[1, pl.ds(odd, 1), :]
                        far[side, at, :] = rows[2, pl.ds(even, 1), :]
                    return 0

                lax.fori_loop(0, tiles, fetch, 0)
            own0 = near[0, pl.ds(PAD, steps_out), :]
            own1 = near[1, pl.ds(PAD, steps_out), :]
            edge0 = near[0, pl.ds(PAD - 1, steps_out), :] + far[0, pl.ds(PAD + 1, steps_out), :]
            edge1 = near[1, pl.ds(PAD - 1, steps_out), :] + far[1, pl.ds(PAD + 1, steps_out), :]
            first = own0 + pltpu.roll(edge0, LANES // 2, 1)
            second = pltpu.roll(own1, LANES // 2, 1) + edge1
            out_ref[pair] = jnp.where(lane < LANES // 2, first, second)


def right_pairs(ids, live, table, weights, steps_out):
    vocab = table.shape[1]
    chans = table.shape[0]
    recipes = live.shape[0]
    vblk = 5 * CHUNK
    vblocks = vocab // vblk
    group = 8
    return pl.pallas_call(
        functools.partial(right_kernel, vocab, vblocks, group, steps_out),
        grid_spec=pltpu.PrefetchScalarGridSpec(
            num_scalar_prefetch=2,
            grid=(vblocks + recipes // group,),
            in_specs=[
                pl.BlockSpec((chans, vblk), lambda s, *_: (0, jnp.minimum(s, vblocks - 1))),
                pl.BlockSpec(weights.shape, lambda s, *_: (0, 0, 0)),
            ],
            out_specs=pl.BlockSpec(
                (group // 2, steps_out, LANES), lambda s, *_: (jnp.maximum(s - vblocks, 0), 0, 0)
            ),
            scratch_shapes=[
                pltpu.VMEM((3, vocab + PAD, LANES), jnp.float32),
                pltpu.VMEM((2, steps_out + 2 * PAD, LANES), jnp.float32),
                pltpu.VMEM((2, steps_out + 2 * PAD, LANES), jnp.float32),
                pltpu.VMEM((3 * LANES, chans), jnp.bfloat16),
            ],
        ),
        out_shape=jax.ShapeDtypeStruct((recipes // 2, steps_out, LANES), jnp.float32),
        compiler_params=pltpu.CompilerParams(vmem_limit_bytes=60 * 1024 * 1024),
        cost_estimate=pl.CostEstimate(
            flops=2 * vocab * chans * 3 * LANES, bytes_accessed=200 * 1024 * 1024, transcendentals=0
        ),
    )(ids, live, table, weights)


TILE = 128
GROUP = 4
BUFS = 4
EARLY = 1


def fused_kernel(
    dp_count, tok_ref, lens, table_hbm, cot_hbm, pa_ref, w_ref, out_ref,
    rows, tbuf, cbuf, lown, lgive, lgot, xout, xin, lfull, evens, odds, operand, tok2, wt, near, far, give, got, rsum,
    xs, xall, gs, gin, dg, dgin, fs, fin, ds, dfin, ids,
    cot_sem, tab_sem, ids_sem, s1_send, s1_recv, s2_send, s2_recv, s3_send, s3_recv, raw_send, raw_recv,
    x_send, x_recv, g_send, g_recv, d_send, d_recv, f_send, f_recv, df_send, df_recv,
):
    f32, bf16 = jnp.float32, jnp.bfloat16
    me = lax.axis_index("tensor")
    blk = lax.axis_index("dp")
    core = me % 2
    sib = me + 1 - 2 * core
    across = (me + 2) % 4
    mesh_ids = pl.DeviceIdType.MESH
    recs, chans, steps = cbuf.shape
    vblk = tbuf.shape[2]
    chunks = table_hbm.shape[1] // vblk
    groups = recs // GROUP
    seq = 2 * steps
    vocab = table_hbm.shape[1]
    width = pa_ref.shape[0]
    feats = width * width

    def remote(src, dst, send, recv, where):
        return pltpu.make_async_remote_copy(
            src_ref=src, dst_ref=dst, send_sem=send, recv_sem=recv, device_id=where, device_id_type=mesh_ids
        )

    def cot_copy(i):
        at = pl.ds(i * GROUP, GROUP)
        return pltpu.make_async_copy(cot_hbm.at[at], cbuf.at[at], cot_sem.at[i])

    def tab_copy(i):
        at = pl.ds(pl.multiple_of(i * vblk, TILE), vblk)
        return pltpu.make_async_copy(table_hbm.at[:, at], tbuf.at[i % BUFS], tab_sem.at[i % BUFS])

    def ids_copy(rec, k):
        return pltpu.make_async_copy(tok2.at[rec], ids.at[k], ids_sem.at[k])

    barrier = pltpu.get_barrier_semaphore()
    for i in range(groups):
        cot_copy(i).start()
    for i in range(BUFS):
        tab_copy(i).start()
    for off in range(1, 4):
        pl.semaphore_signal(barrier, inc=1, device_id={"tensor": (me + off) % 4}, device_id_type=mesh_ids)
    for off in range(1, dp_count):
        pl.semaphore_signal(barrier, inc=1, device_id={"dp": (blk + off) % dp_count}, device_id_type=mesh_ids)
    spot = lax.broadcasted_iota(jnp.int32, (1, seq), 1)
    for rec in range(recs):
        tok2[rec:rec + 1, :] = jnp.where(spot < lens[rec], tok_ref[rec:rec + 1, :] * 2, 2 * vocab)
    for k in range(GROUP):
        ids_copy(k, k).start()

    def s1(i):
        return remote(lgive.at[i], lgot.at[i], s1_send.at[i], s1_recv.at[i], {"tensor": sib})

    def s2(i):
        return remote(xout.at[i], xin.at[i], s2_send.at[i], s2_recv.at[i], {"tensor": across})

    def s3(i):
        here = lfull.at[2 * i + core]
        return remote(here, here, s3_send.at[i], s3_recv.at[i], {"tensor": sib})

    def s3_in(i):
        there = lfull.at[2 * i + 1 - core]
        return remote(there, there, s3_send.at[i], s3_recv.at[i], {"tensor": sib})

    lane = lax.broadcasted_iota(jnp.int32, (width, steps), 1)

    for side, pairs in enumerate((((2, 0), (None, 4)), ((3, 1), (None, None)))):
        for col, halves in enumerate(pairs):
            block = [jnp.zeros((width, chans), bf16) if tap is None else w_ref[tap] for tap in halves]
            wt[side * chans:(side + 1) * chans, col * TILE:(col + 1) * TILE] = jnp.concatenate(block, axis=0).T
    near[...] = jnp.zeros(near.shape, f32)
    far[...] = jnp.zeros(far.shape, f32)
    rows[pl.ds(2 * vocab, 8), :] = jnp.zeros((8, TILE), f32)

    def left_step(i):
        cot_copy(i).wait()
        for dst, pair in ((lgive, 2 * i + 1 - core), (lown, 2 * i + core)):
            for s in range(2):
                rec = 2 * pair + s
                part = jnp.dot(pa_ref[...], cbuf[rec], preferred_element_type=f32)
                dst[i, s * width:(s + 1) * width, :] = jnp.where(2 * lane < lens[rec], part, 0.0)

    def chip_step(i):
        s1(i).wait_recv()
        both = lown[i] + lgot[i]
        lown[i] = both
        xout[i] = both.astype(bf16)
        s2(i).start()

    def turn(i):
        tab_copy(i).wait()
        slot = i % BUFS
        for j in range(vblk // TILE):
            base = pl.multiple_of(2 * (i * vblk + j * TILE), 2 * TILE)
            for h in range(2):
                part = tbuf[slot, h * TILE:(h + 1) * TILE, j * TILE:(j + 1) * TILE]
                rows[pl.ds(base + h, TILE, stride=2), :] = part.T.astype(f32)

        @pl.when(i + BUFS < chunks)
        def _():
            tab_copy(i + BUFS).start()


    def each(step):
        def body(i, _):
            step(i)
            return 0

        return body

    lax.fori_loop(0, groups, each(left_step), 0)
    lax.fori_loop(0, EARLY, each(turn), 0)
    pl.semaphore_wait(barrier, 3 + dp_count - 1)
    for i in range(groups):
        s1(i).start()
    lax.fori_loop(EARLY, EARLY + 2, each(turn), 0)
    lax.fori_loop(0, groups // 2, each(chip_step), 0)

    def late_turn(i):
        turn(i)

        @pl.when(i == EARLY + 2)
        def _():
            lax.fori_loop(groups // 2, groups, each(chip_step), 0)

    lax.fori_loop(EARLY + 2, chunks, each(late_turn), 0)

    def finish_left(i):
        s2(i).wait_recv()
        lfull[2 * i + core] = lown[i] + xin[i].astype(f32)
        s3(i).start()

    finish_left(0)

    def gather(k):
        for t in range(steps):
            evens[k, 2 * t:2 * t + 2, :] = rows[pl.ds(ids[k, 2 * t], 2), :]
            odds[k, 2 * t:2 * t + 2, :] = rows[pl.ds(ids[k, 2 * t + 1], 2), :]

    upper = lax.broadcasted_iota(jnp.int32, (steps, TILE), 1) >= TILE // 2
    upper_rows = lax.broadcasted_iota(jnp.int32, (8, TILE), 1) >= TILE // 2

    def project(g):
        for k in range(GROUP):
            for n, buf in enumerate((evens, odds)):
                for h in range(2):
                    col = (2 * n + h) * TILE
                    operand[k * steps:(k + 1) * steps, col:col + TILE] = buf[k, pl.ds(h, steps, stride=2), :].astype(bf16)
        from_even = jnp.dot(operand[:, :chans], wt[:chans], preferred_element_type=f32)
        from_odd = jnp.dot(operand[:, chans:], wt[chans:, :TILE], preferred_element_type=f32)
        for k in range(GROUP):
            at = slice(k * steps, (k + 1) * steps)
            near[k, pl.ds(PAD, steps), :] = from_even[at, :TILE] + from_odd[at]
            far[k, pl.ds(PAD, steps), :] = from_even[at, TILE:]
        for k in range(GROUP):
            edge = near[k, pl.ds(PAD - 1, steps), :] + far[k, pl.ds(PAD + 1, steps), :]
            mixed = jnp.where(upper, edge, near[k, pl.ds(PAD, steps), :])
            right = mixed + pltpu.roll(mixed, TILE // 2, 1)
            high = right.astype(bf16).astype(f32)
            right = jnp.where(upper, right - high, high).astype(bf16)
            left = lfull[2 * g + k // 2, (k % 2) * width:(k % 2 + 1) * width, :]
            left_high = left.astype(bf16)
            left = jnp.concatenate([left_high, (left - left_high.astype(f32)).astype(bf16)], axis=0)
            raw = jnp.dot(left, right, preferred_element_type=f32)
            raw = raw[:width] + raw[width:]
            raw = raw + pltpu.roll(raw, TILE // 2, 1)
            for j in range(4):
                lo = 16 * j
                give[j, g * GROUP + k] = jnp.where(upper_rows, raw[lo + 8:lo + 16], raw[lo:lo + 8])

    def raw_copy(g, off):
        peer = (me + off) % 4
        at = pl.ds(g * GROUP, GROUP)
        return remote(
            give.at[peer, at], got.at[off - 1, at], raw_send.at[off - 1, g], raw_recv.at[off - 1, g], {"tensor": peer}
        )

    offs = range(1, dp_count)

    def x_copy(c, off):
        peer = (blk + off) % dp_count
        at = pl.ds(pl.multiple_of(c * 8, 8), 8)
        return remote(
            xs.at[peer, at], xall.at[blk, at], x_send.at[off - 1, c], x_recv.at[off - 1, c], {"dp": peer}
        )

    def ship(c):
        for g in (2 * c, 2 * c + 1):
            for off in range(1, 4):
                raw_copy(g, off).wait_recv()
        at = pl.ds(pl.multiple_of(c * 8, 8), 8)
        base = pl.multiple_of(c * 64, 64)
        raw = (give[me, at] + got[0, at]) + (got[1, at] + got[2, at])
        rsum[pl.ds(base, 64), :] = raw.reshape(64, TILE)
        for p in range(dp_count):
            xs[p, at, :] = rsum[pl.ds(base + p, 8, stride=8), :]
        xall[blk, at, :] = xs[blk, at, :]
        for off in offs:
            x_copy(c, off).start()

    def group_step(g, _):
        for k in range(GROUP):
            ids_copy(g * GROUP + k, k).wait()
            gather(k)

            @pl.when(g < groups - 1)
            def _():
                ids_copy((g + 1) * GROUP + k, k).start()

        @pl.when(g < groups - 1)
        def _():
            finish_left(g + 1)

        s3_in(g).wait_recv()
        project(g)
        for off in range(1, 4):
            raw_copy(g, off).start()
        return 0

    lax.fori_loop(0, groups, group_step, 0)
    parts = recs // 8
    for c in range(parts):
        ship(c)
    for c in range(parts):
        for off in offs:
            x_copy(c, off).wait_recv()
    every = xall[...].reshape(dp_count * recs, TILE)
    high = every.astype(bf16)
    low = (every - high.astype(f32)).astype(bf16)
    gram = lax.dot_general(
        jnp.concatenate([high, high, low], axis=1), jnp.concatenate([high, low, high], axis=1),
        (((1,), (1,)), ((), ())), preferred_element_type=f32,
    )
    out_rows = recs // 4
    for j in range(4):
        starts = [d * recs + j * out_rows for d in range(dp_count)]
        gs[j] = jnp.concatenate([gram[at:at + out_rows] for at in starts], axis=0).astype(bf16)
    count = dp_count * recs
    row_id = lax.broadcasted_iota(jnp.int32, (count, count), 0)
    col_id = lax.broadcasted_iota(jnp.int32, (count, count), 1)
    rounded = gram.astype(bf16).astype(f32)
    dg[...] = jnp.sum(jnp.where(row_id == col_id, rounded, 0.0), axis=0, keepdims=True)

    def g_copy(off):
        peer = (me + off) % 4
        return remote(gs.at[peer], gin.at[off - 1], g_send.at[off - 1], g_recv.at[off - 1], {"tensor": peer})

    def d_copy(off):
        return remote(dg, dgin.at[off - 1], d_send.at[off - 1], d_recv.at[off - 1], {"tensor": (me + off) % 4})

    for off in range(1, 4):
        g_copy(off).start()
        d_copy(off).start()
    mine = gs[me].astype(f32)
    squares = dg[...]
    for off in range(1, 4):
        g_copy(off).wait_recv()
        d_copy(off).wait_recv()
        mine = mine + gin[off - 1].astype(f32)
        squares = squares + dgin[off - 1]
    for d in range(dp_count):
        fs[d] = mine[d * out_rows:(d + 1) * out_rows]
    ds[...] = squares

    def f_copy(off):
        peer = (blk + off) % dp_count
        return remote(fs.at[peer], fin.at[off - 1], f_send.at[off - 1], f_recv.at[off - 1], {"dp": peer})

    def df_copy(off):
        return remote(
            ds, dfin.at[off - 1], df_send.at[off - 1], df_recv.at[off - 1], {"dp": (blk + off) % dp_count}
        )

    for off in offs:
        f_copy(off).start()
        df_copy(off).start()
    total = fs[blk]
    for off in offs:
        f_copy(off).wait_recv()
        df_copy(off).wait_recv()
        total = total + fin[off - 1]
        squares = squares + dfin[off - 1]
    scale = lax.rsqrt(squares * (1.0 / feats) + 1e-06)
    own_row = lax.broadcasted_iota(jnp.int32, (out_rows, count), 0) + (blk * recs + me * out_rows)
    own_col = lax.broadcasted_iota(jnp.int32, (out_rows, count), 1)
    row_scale = jnp.sum(jnp.where(own_row == own_col, scale, 0.0), axis=1, keepdims=True)
    out_ref[...] = total * scale * row_scale

    def sent(i, _):
        s1(i).wait_send()
        s2(i).wait_send()
        s3(i).wait_send()
        for off in range(1, 4):
            raw_copy(i, off).wait_send()
        return 0

    lax.fori_loop(0, groups, sent, 0)
    for off in offs:
        for c in range(parts):
            x_copy(c, off).wait_send()
        f_copy(off).wait_send()
        df_copy(off).wait_send()
    for off in range(1, 4):
        g_copy(off).wait_send()
        d_copy(off).wait_send()


def fused(ids, lengths, table, cotangent, proj_a, weights, dp_count):
    recs, chans, steps = cotangent.shape
    width = proj_a.shape[0]
    vocab = table.shape[1]
    groups = recs // GROUP
    count = dp_count * recs
    f32, bf16 = jnp.float32, jnp.bfloat16
    dma = pltpu.SemaphoreType.DMA
    hbm = pl.BlockSpec(memory_space=pl.ANY)
    vmem = pl.BlockSpec(memory_space=pltpu.VMEM)
    smem = pl.BlockSpec(memory_space=pltpu.SMEM)
    tokens = pltpu.VMEM((GROUP, 2 * steps, TILE), f32)
    padded = pltpu.VMEM((GROUP, steps + 2 * PAD, TILE), f32)
    lefts = pltpu.VMEM((groups, 2 * width, steps), f32)
    lefts_half = pltpu.VMEM((groups, 2 * width, steps), bf16)
    others = dp_count - 1
    return pl.pallas_call(
        functools.partial(fused_kernel, dp_count),
        out_shape=pltpu.VMEM((recs // 4, count), f32),
        in_specs=[vmem, smem, hbm, hbm, vmem, vmem],
        out_specs=vmem,
        scratch_shapes=[
            pltpu.VMEM((2 * vocab + 8, TILE), f32),
            pltpu.VMEM((BUFS, chans, vocab // 10), bf16),
            pltpu.VMEM((recs, chans, steps), bf16),
            lefts, lefts, lefts, lefts_half, lefts_half,
            pltpu.VMEM((2 * groups, 2 * width, steps), f32),
            tokens, tokens,
            pltpu.VMEM((GROUP * steps, 4 * TILE), bf16),
            pltpu.VMEM((recs, 2 * steps), jnp.int32),
            pltpu.VMEM((2 * chans, 2 * TILE), bf16),
            padded, padded,
            pltpu.VMEM((4, recs, 8, TILE), f32),
            pltpu.VMEM((3, recs, 8, TILE), f32),
            pltpu.VMEM((recs * 8, TILE), f32),
            pltpu.VMEM((dp_count, recs, TILE), f32),
            pltpu.VMEM((dp_count, recs, TILE), f32),
            pltpu.VMEM((4, count // 4, count), bf16),
            pltpu.VMEM((3, count // 4, count), bf16),
            pltpu.VMEM((1, count), f32),
            pltpu.VMEM((3, 1, count), f32),
            pltpu.VMEM((dp_count, recs // 4, count), f32),
            pltpu.VMEM((others, recs // 4, count), f32),
            pltpu.VMEM((1, count), f32),
            pltpu.VMEM((others, 1, count), f32),
            pltpu.SMEM((GROUP, 2 * steps), jnp.int32),
            dma((groups,)), dma((BUFS,)), dma((GROUP,)),
            dma((groups,)), dma((groups,)), dma((groups,)), dma((groups,)), dma((groups,)), dma((groups,)),
            dma((3, groups)), dma((3, groups)),
            dma((others, recs // 8)), dma((others, recs // 8)), dma((3,)), dma((3,)), dma((3,)), dma((3,)),
            dma((others,)), dma((others,)), dma((others,)), dma((others,)),
        ],
        compiler_params=pltpu.CompilerParams(
            collective_id=0, has_side_effects=True, vmem_limit_bytes=56 * 1024 * 1024
        ),
        cost_estimate=pl.CostEstimate(flops=6 * 10**9, bytes_accessed=20 * 2**20, transcendentals=0),
    )(ids, lengths, table, cotangent, proj_a, weights)


def left_part_of(lengths, cotangent, proj_a):
    steps_out = cotangent.shape[2]
    outpos = 2 * jnp.arange(steps_out, dtype=jnp.int32)
    tkeep = outpos[None, :] < lengths[:, None]
    masked = jnp.where(tkeep[:, None, :], cotangent, jnp.zeros((), cotangent.dtype))
    return jnp.einsum("nct,ca->nat", masked, proj_a, preferred_element_type=jnp.float32)


def local(token_ids, lengths, table, cotangent, proj_a, proj_b):
    recipes_here, seqlen = token_ids.shape
    chans, width = proj_a.shape
    vocab = table.shape[1]
    steps_out = seqlen // 2
    total_feats = width * width
    if lax.axis_size("tensor") == 4 and lax.axis_size("dp") == 8:
        raw = fused(token_ids, lengths, table, cotangent, proj_a.T, jnp.transpose(proj_b, (1, 2, 0)), 8)
        return raw * (1.0 / total_feats)
    left_part = left_part_of(lengths, cotangent, proj_a)

    pos = jnp.arange(seqlen, dtype=jnp.int32)
    ids = jnp.where(pos[None, :] < lengths[:, None], token_ids, vocab).reshape(-1)
    live = (lengths + 1) // 2
    weights = jnp.transpose(proj_b, (1, 2, 0))
    left_own = lax.psum_scatter(left_part, "tensor", scatter_dimension=0, tiled=True)
    right_part = right_pairs(ids, live, table, weights, steps_out)
    right_own = lax.psum_scatter(right_part, "tensor", scatter_dimension=0, tiled=True)
    mine = right_own.shape[0] * 2
    left_two = left_own.reshape(mine // 2, 2, width, steps_out)
    raw = jnp.stack(
        [
            jnp.einsum(
                "nat,ntb->nab", left_two[:, side], right_own[:, :, side * width:(side + 1) * width],
                precision=lax.Precision.HIGHEST,
            )
            for side in range(2)
        ],
        axis=1,
    ).reshape(mine, total_feats)
    scale = lax.rsqrt(jnp.mean(raw * raw, axis=1) + 1e-06)
    unit = (raw * scale[:, None]).astype(jnp.bfloat16)
    every = lax.all_gather(unit, ("dp", "tensor"), axis=0, tiled=True)
    terms = lax.dot_general(
        unit, every, (((1,), (1,)), ((), ())), preferred_element_type=jnp.float32
    )
    return terms * (1.0 / total_feats)


def solution(mesh):
    placed = (
        P("dp", None),
        P("dp"),
        P("tensor", None),
        P("dp", "tensor", None),
        P("tensor", None),
        P("tensor", None, None),
    )
    return jax.shard_map(
        local, mesh=mesh, in_specs=placed, out_specs=P(("dp", "tensor"), None), check_vma=False
    )
```
